512 devices in a mesh: segment: 2 (over core), seq: 32 (over x, z_lo), mp: 8 (over z_hi, y).
Axes of the slice: x: 4, y: 4, z: 16 (z_hi: 2, z_lo: 8; z = z_hi * 8 + z_lo), core: 2. Of those that a mesh axis runs over, the one named last changes fastest.
Arguments:
- hidden: bfloat16 [2, 2, 5120, 2048], P('segment', None, 'seq', 'mp'), may hold values from -120 to 120
- memory: bfloat16 [2, 2, 5120, 2048], P('segment', None, 'seq', 'mp'), may hold values from -120 to 120
- w_query: bfloat16 [2, 2048, 2048], P('segment', None, 'mp'), may hold values from -1 to 1
- w_key: bfloat16 [2, 2048, 2048], P('segment', None, 'mp'), may hold values from -4 to 4
- w_value: bfloat16 [2, 2048, 2048], P('segment', None, 'mp'), may hold values from -0.125 to 0.125
- w_out: bfloat16 [2, 2048, 2048], P('segment', 'mp'), may hold values from -3 to 3
- norm_gain: float32 [2, 2048], P('segment'), may hold values from 0.1 to 1.9
- final_gain: float32 [2048], replicated, may hold values from 0.1 to 1.9
- lengths: int32 [2, 2, 2], P('segment'), may hold values from 2560 to 5120, as said below
Outputs:
- sublayer: bfloat16 [2, 2, 5120, 2048], P('segment', None, 'seq', 'mp')
The draws below stay inside these ranges and needn't reach their ends.
Inputs may be any that keep to these rules, and one draw needn't show every extreme that they name: For each sequence b: lengths[0, b, 0] equals lengths[0, b, 1] (the encoder's document length); lengths[1, b, 0] is the target length and lengths[1, b, 1] the length of the document whose memory the decoder reads; one of these three lengths equals 5120.
All inputs are finite; a program needn't handle non-finite values.
Results may differ from the reference program's by a relative error of at most 0.018.
Values may be sent and summed in bfloat16 or wider, within the bound.
A program may use at most 128 MiB of HBM per device.

```python
import math
import jax
import jax.numpy as jnp
from jax import lax

D = 2048
HEADS = 32
DH = 64
SEQS = 2
LEN = 5120


def states(seed_key):
    key_one = jax.random.fold_in(jax.random.fold_in(seed_key, 11), 0)
    key_three = jax.random.fold_in(jax.random.fold_in(seed_key, 11), 2)
    key_four = jax.random.fold_in(jax.random.fold_in(seed_key, 11), 3)
    full_shape = (3, SEQS, LEN, D)
    raw_draw = jnp.clip(jax.random.normal(key_one, full_shape, jnp.float32), -6.0, 6.0)
    row_scale = jnp.exp(jax.random.uniform(key_three, (3, SEQS, LEN, 1), jnp.float32, math.log(0.3), math.log(3.0)))
    col_scale = jnp.exp(jax.random.uniform(key_four, (3, 1, 1, D), jnp.float32, math.log(0.5), math.log(5.0)))
    drawn = raw_draw * row_scale * col_scale
    return jnp.clip(drawn, -120.0, 120.0)


def draw_hidden(key, part):
    drawn = states(key)
    return jnp.stack([drawn[0], drawn[1]]).astype(jnp.bfloat16)


def draw_memory(key, part):
    drawn = states(key)
    return jnp.stack([drawn[2], jnp.flip(drawn[2], axis=1)]).astype(jnp.bfloat16)


def query_key(seed_key):
    key_one, key_two = jax.random.split(jax.random.fold_in(seed_key, 23), 2)
    column_count = HEADS * DH
    full_shape = (2, D, column_count)
    weight_query = jnp.clip(jax.random.normal(key_one, full_shape, jnp.float32), -6.0, 6.0) / math.sqrt(D)
    weight_key = jnp.clip(jax.random.normal(key_two, full_shape, jnp.float32), -6.0, 6.0) / math.sqrt(D)
    return (weight_query, weight_key)


def draw_w_query(key, part):
    return query_key(key)[0].astype(jnp.bfloat16)


def draw_w_key(key, part):
    return query_key(key)[1].astype(jnp.bfloat16)


def draw_lengths(key, part):
    key_one, key_two = jax.random.split(jax.random.fold_in(key, 37), 2)
    drawn = jax.random.randint(key_one, (SEQS, 3), LEN // 2, LEN + 1)
    chosen = jax.random.randint(key_two, (SEQS, 1), 0, 3)
    drawn = jnp.where(jnp.arange(3)[None, :] == chosen, LEN, drawn)
    encoder_pair = jnp.stack([drawn[:, 0], drawn[:, 0]], axis=1)
    decoder_pair = jnp.stack([drawn[:, 1], drawn[:, 2]], axis=1)
    return jnp.stack([encoder_pair, decoder_pair]).astype(jnp.int32)


def steps_of(own_key, shape, cuts, least, high):
    def one(position, blocks):
        heights = jax.random.uniform(jax.random.fold_in(jax.random.fold_in(own_key, 6), position), (blocks,), jnp.float32, least / len(cuts), high / len(cuts))
        return jnp.repeat(jnp.exp(heights), shape[position] // blocks).reshape((-1,) + (1,) * (len(shape) - position - 1))

    level = one(*cuts[0])
    for cut in cuts[1:]:
        level = level * one(*cut)
    return level


def centred(stream_key, extent, deviation, bound, pieces=(), kind=jnp.bfloat16):
    array = jax.random.normal(stream_key, extent, jnp.float32) * deviation
    if len(pieces) > 0:
        array = steps_of(stream_key, extent, pieces, -0.22, 0.18) * array
    return jnp.clip(array, min=-bound, max=bound).astype(kind)


def setup_inputs(seed: int = 0) -> dict:
    key_of = jax.random.split(jax.random.key(seed), 10)
    hidden = draw_hidden(jax.random.fold_in(key_of[9], 71), 0)
    memory = draw_memory(jax.random.fold_in(key_of[9], 71), 0)
    w_query = draw_w_query(jax.random.fold_in(key_of[9], 71), 0)
    w_key = draw_w_key(jax.random.fold_in(key_of[9], 71), 0)
    w_value = centred(key_of[4], (2, D, HEADS * DH), D ** -0.5, 0.125, ((0, 2), (2, 8)))
    w_out = centred(key_of[5], (2, HEADS * DH, D), 0.5, 3.0, ((0, 2), (1, 8)))
    norm_gain = jnp.clip(1.0 + 0.18 * jax.random.normal(key_of[6], (2, D), jnp.float32), 0.1, 1.9)
    final_gain = jnp.clip(1.0 + 0.18 * jax.random.normal(key_of[7], (D,), jnp.float32), 0.1, 1.9)
    lengths = draw_lengths(jax.random.fold_in(key_of[9], 71), 0)
    return {"hidden": hidden, "memory": memory, "w_query": w_query, "w_key": w_key, "w_value": w_value, "w_out": w_out, "norm_gain": norm_gain, "final_gain": final_gain, "lengths": lengths}


def normalize(values, gain_row):
    widened = values.astype(jnp.float32)
    square = lax.optimization_barrier(jnp.mean(widened * widened, axis=-1, keepdims=True))
    return (widened * lax.rsqrt(square + 1e-06) * gain_row.astype(jnp.float32)).astype(jnp.bfloat16)

def attend_head(query_head, key_head, value_head, key_length):
    block_size = math.gcd(LEN, 1024)
    visible = jnp.arange(LEN) < key_length
    query_blocks = query_head.reshape(LEN // block_size, block_size, DH)

    def one_block(query_block):
        scores = jnp.dot(query_block, key_head.T, preferred_element_type=jnp.float32) * 0.25
        scores = jnp.where(visible[None, :], scores, -1e+30)
        largest = lax.optimization_barrier(jnp.max(scores, axis=-1, keepdims=True))
        exponent = jnp.where(visible[None, :], jnp.exp(scores - largest), 0.0)
        totals = lax.optimization_barrier(jnp.sum(exponent, axis=-1, keepdims=True))
        weighted = jnp.dot(exponent.astype(jnp.bfloat16), value_head, preferred_element_type=jnp.float32)
        return weighted / totals
    return lax.map(one_block, query_blocks).reshape(LEN, DH)

def section(query_src, key_src, query_gain, key_gain, weight_query, weight_key, weight_value, weight_out, length_pair):
    query_in = normalize(query_src, query_gain)
    key_in = normalize(key_src, key_gain)
    queries = jnp.dot(query_in, weight_query, preferred_element_type=jnp.float32).astype(jnp.bfloat16)
    keys = jnp.dot(key_in, weight_key, preferred_element_type=jnp.float32).astype(jnp.bfloat16)
    values = jnp.dot(key_in, weight_value, preferred_element_type=jnp.float32).astype(jnp.bfloat16)
    query_heads = queries.reshape(LEN, HEADS, DH).transpose(1, 0, 2)
    key_heads = keys.reshape(LEN, HEADS, DH).transpose(1, 0, 2)
    value_heads = values.reshape(LEN, HEADS, DH).transpose(1, 0, 2)
    key_length = length_pair[1]

    def per_head(triple):
        return attend_head(triple[0], triple[1], triple[2], key_length)
    context = lax.map(per_head, (query_heads, key_heads, value_heads))
    context = context.transpose(1, 0, 2).reshape(LEN, HEADS * DH)
    positions = jnp.arange(LEN)
    context = jnp.where((positions < length_pair[0])[:, None], context, 0.0).astype(jnp.bfloat16)
    branch = jnp.dot(context, weight_out, preferred_element_type=jnp.float32)
    return (query_src.astype(jnp.float32) + branch).astype(jnp.bfloat16)

def reference(hidden, memory, w_query, w_key, w_value, w_out, norm_gain, final_gain, lengths):
    encoder_out = jnp.stack([section(hidden[0, index], hidden[0, index], norm_gain[0], norm_gain[0], w_query[0], w_key[0], w_value[0], w_out[0], lengths[0, index]) for index in range(SEQS)])
    decoder_out = jnp.stack([section(hidden[1, index], memory[0, index], norm_gain[1], final_gain, w_query[1], w_key[1], w_value[1], w_out[1], lengths[1, index]) for index in range(SEQS)])
    return jnp.stack([encoder_out, decoder_out])
```

```python
import functools
import math

import jax
import jax.numpy as jnp
from jax import lax
from jax.experimental import pallas as pl
from jax.experimental.pallas import tpu as pltpu
from jax.sharding import PartitionSpec as P

DH = 64
NX, NZ, NH, NY = 4, 8, 2, 4
LANES = 128
BF = jnp.bfloat16
F32 = jnp.float32
VMEM_LIMIT = 48 * 1024 * 1024


def place():
    seg, seq, mp = lax.axis_index("segment"), lax.axis_index("seq"), lax.axis_index("mp")
    return seg, seq // NZ, seq % NZ, mp // NY, mp % NY


def at(seg, x, zl, zh, y):
    return (seg, x * NZ + zl, zh * NY + y)


def push(src, dst, send, recv, device):
    return pltpu.make_async_remote_copy(
        src_ref=src, dst_ref=dst, send_sem=send, recv_sem=recv,
        device_id=device, device_id_type=pl.DeviceIdType.MESH,
    )


def greet(partners):
    barrier = pltpu.get_barrier_semaphore()
    for device in partners:
        pl.semaphore_signal(barrier, inc=1, device_id=device, device_id_type=pl.DeviceIdType.MESH)
    pl.semaphore_wait(barrier, len(partners))


def low_lanes(shape):
    return lax.broadcasted_iota(jnp.int32, shape, 1) < DH


def swap(tile):
    return pltpu.roll(tile, DH, 1)


def merge(low, high):
    return jnp.where(low_lanes(low.shape), low, high)


def gather_kernel(
    h_ref, m_ref, wq_ref, wk_ref, wv_ref, gain_ref,
    qa_ref, kva_ref,
    xs, qs, kvs, accq, acck, accv, ssq,
    own_send, mem_send, fwd_send, x_recv, z_send, z_recv, kv_send, kv_recv,
):
    seg, x, zl, zh, y = place()
    mp = zh * NY + y
    other = (NH - 1 - zh) * NY + y
    total, chunk = h_ref.shape
    rows = kvs.shape[1]
    batch = total // rows
    heads = accq.shape[1] // DH
    width = chunk * NH * NY

    here = [(zh, (y + k) % NY) for k in range(1, NY)]
    group = [(NH - 1 - zh, y)] + here
    partners = [at(seg, x, zl, a, b) for a, b in group]
    partners += [at(1 - seg, x, zl, a, b) for a, b in group] + [at(1 - seg, x, zl, zh, y)]
    partners += [at(seg, x, (zl + k) % NZ, zh, y) for k in range(1, NZ)]
    partners += [at(seg, (x + k) % NX, zl, zh, y) for k in range(1, NX)]
    greet(partners)

    def own_copies():
        return [
            push(h_ref, xs.at[0, mp], own_send.at[k], x_recv.at[0, mp], at(seg, x, zl, a, b))
            for k, (a, b) in enumerate(group)
        ]

    def memory_copies():
        return [
            push(m_ref, xs.at[1, mp], mem_send.at[k], x_recv.at[1, mp], at(1, x, zl, a, b))
            for k, (a, b) in enumerate(group + [(zh, y)])
        ]

    def forwards(array):
        return [
            push(xs.at[array, other], xs.at[array, other], fwd_send.at[array, k], x_recv.at[array, other],
                 at(seg, x, zl, a, b))
            for k, (a, b) in enumerate(here)
        ]

    def arrived(array, c):
        push(xs.at[array, c], xs.at[array, c], fwd_send.at[array, 0], x_recv.at[array, c],
             at(seg, x, zl, zh, y)).wait_recv()

    for copy in own_copies():
        copy.start()

    @pl.when(seg == 0)
    def _():
        for copy in memory_copies():
            copy.start()

    xs[0, mp] = h_ref[...]
    accq[...] = jnp.zeros_like(accq)
    acck[...] = jnp.zeros_like(acck)
    accv[...] = jnp.zeros_like(accv)
    ssq[...] = jnp.zeros_like(ssq)

    def chunk_step(j, carry):
        c = (zh + j // NY) % NH * NY + (y + j % NY) % NY

        @pl.when(j > 0)
        def _():
            arrived(0, c)

        @pl.when(j == NY)
        def _():
            for copy in forwards(0):
                copy.start()

        @pl.when(seg == 1)
        def _():
            arrived(1, c)

            @pl.when(j == NY)
            def _():
                for copy in forwards(1):
                    copy.start()

        cols = pl.ds(pl.multiple_of(c * chunk, chunk), chunk)
        xq = xs[0, c].astype(F32)
        ssq[0] += jnp.sum(xq * xq, axis=1, keepdims=True)
        accq[...] += jnp.dot(
            (xq * gain_ref[0:1, cols]).astype(BF), wq_ref[cols, :], preferred_element_type=F32
        )
        xk = xs[seg, c].astype(F32)
        ssq[1] += jnp.sum(xk * xk, axis=1, keepdims=True)
        xk = (xk * gain_ref[1:2, cols]).astype(BF)
        acck[...] += jnp.dot(xk, wk_ref[cols, :], preferred_element_type=F32)
        accv[...] += jnp.dot(xk, wv_ref[cols, :], preferred_element_type=F32)
        return carry

    lax.fori_loop(0, NH * NY, chunk_step, 0)

    rq = lax.rsqrt(ssq[0, :, 0:1] / width + 1e-06)
    rk = lax.rsqrt(ssq[1, :, 0:1] / width + 1e-06)
    half = rows // 2
    for b in range(batch):
        span = slice(b * rows, (b + 1) * rows)
        for t in range(heads // 2):
            tile = slice(t * LANES, (t + 1) * LANES)
            k = acck[span, tile] * rk[span]
            v = accv[span, tile] * rk[span]
            q = accq[span, tile] * rq[span]
            first = b * heads + 2 * t
            kvs[first] = merge(k, swap(v)).astype(BF)
            kvs[first + 1] = merge(swap(k), v).astype(BF)
            qs[first] = merge(q[:half], swap(q[half:])).astype(BF)
            qs[first + 1] = merge(swap(q[:half]), q[half:]).astype(BF)

    def z_copies(k):
        z = (zl + k) % NZ
        device = at(seg, x, z, zh, y)
        return (
            push(kvs.at[z], kva_ref.at[x, zl], z_send.at[0, k], kv_recv.at[x, zl], device),
            push(qs.at[z], qa_ref.at[zl], z_send.at[1, k], z_recv.at[zl], device),
        )

    def z_start(k, carry):
        for copy in z_copies(k):
            copy.start()
        return carry

    lax.fori_loop(1, NZ, z_start, 0)
    kva_ref[x, zl] = kvs[zl]
    qa_ref[zl] = qs[zl]

    def x_copy(k, z):
        return push(kva_ref.at[x, z], kva_ref.at[x, z], kv_send.at[k, z], kv_recv.at[x, z],
                    at(seg, (x + k) % NX, zl, zh, y))

    def kv_arrived(xx, z):
        push(kva_ref.at[xx, z], kva_ref.at[xx, z], kv_send.at[0, 0], kv_recv.at[xx, z],
             at(seg, x, zl, zh, y)).wait_recv()

    def x_start(k, carry):
        z = (zl + NZ - k) % NZ

        @pl.when(k > 0)
        def _():
            kv_arrived(x, z)

        for step in range(1, NX):
            x_copy(step, z).start()
        return carry

    lax.fori_loop(0, NZ, x_start, 0)

    def x_wait(k, carry):
        z = (zl + NZ - k) % NZ
        for step in range(1, NX):
            kv_arrived((x + step) % NX, z)

        @pl.when(k > 0)
        def _():
            push(qa_ref.at[z], qa_ref.at[z], z_send.at[1, 0], z_recv.at[z], at(seg, x, zl, zh, y)).wait_recv()
            for copy in z_copies(k):
                copy.wait_send()

        for step in range(1, NX):
            x_copy(step, z).wait_send()
        return carry

    lax.fori_loop(0, NZ, x_wait, 0)

    for copy in own_copies() + forwards(0):
        copy.wait_send()

    @pl.when(seg == 0)
    def _():
        for copy in memory_copies():
            copy.wait_send()

    @pl.when(seg == 1)
    def _():
        for copy in forwards(1):
            copy.wait_send()


def gather(hidden, memory, w_query, w_key, w_value, gains, rows):
    total, chunk = hidden.shape
    cols = w_query.shape[1]
    parts = NH * NY
    dma = pltpu.SemaphoreType.DMA
    vmem = pl.BlockSpec(memory_space=pltpu.VMEM)
    return pl.pallas_call(
        gather_kernel,
        out_shape=(
            jax.ShapeDtypeStruct((NZ, rows // 2, LANES), BF),
            jax.ShapeDtypeStruct((NX, NZ, rows, LANES), BF),
        ),
        in_specs=[vmem] * 6,
        out_specs=(vmem, vmem),
        scratch_shapes=[
            pltpu.VMEM((2, parts, total, chunk), BF),
            pltpu.VMEM((NZ, rows // 2, LANES), BF),
            pltpu.VMEM((NZ, rows, LANES), BF),
            pltpu.VMEM((total, cols), F32),
            pltpu.VMEM((total, cols), F32),
            pltpu.VMEM((total, cols), F32),
            pltpu.VMEM((2, total, LANES), F32),
            dma((NY,)),
            dma((NY + 1,)),
            dma((2, NY)),
            dma((2, parts)),
            dma((2, NZ)),
            dma((NZ,)),
            dma((NX, NZ)),
            dma((NX, NZ)),
        ],
        compiler_params=pltpu.CompilerParams(
            collective_id=1, has_side_effects=True, vmem_limit_bytes=VMEM_LIMIT
        ),
        name="gather",
    )(hidden, memory, w_query, w_key, w_value, gains)


def attend_kernel(limits, qa_ref, kv_ref, out_ref, keys, scores):
    step = pl.program_id(0)
    count = kv_ref.shape[0]
    sources, half, _ = qa_ref.shape
    block = scores.shape[0]
    pieces = 5

    @pl.when(step == 0)
    def _():
        keys[:, :LANES] = kv_ref[...]
        row = lax.broadcasted_iota(jnp.int32, (count, LANES), 0)
        lane = lax.broadcasted_iota(jnp.int32, (count, LANES), 1)
        bias = jnp.where(row < limits[1], 0.0, -1e30)
        keys[:, LANES:] = jnp.where(lane == 0, bias, jnp.where(lane == 1, 1.0, 0.0)).astype(BF)

    parts = []
    for s in range(sources):
        packed = qa_ref[s].astype(F32)
        parts += [merge(packed, jnp.zeros_like(packed)), merge(swap(packed), jnp.zeros_like(packed))]
    query = jnp.concatenate(parts, axis=0).astype(BF)
    flag = (lax.broadcasted_iota(jnp.int32, (block, LANES), 1) == 0).astype(BF)
    query = jnp.concatenate([query, flag], axis=1)

    size = count // pieces
    top = None
    for i in range(pieces):
        part = lax.dot_general(
            query, keys[i * size:(i + 1) * size, :], (((1,), (1,)), ((), ())), preferred_element_type=F32
        )
        scores[:, i * size:(i + 1) * size] = part
        high = jnp.max(part, axis=1, keepdims=True)
        top = high if top is None else jnp.maximum(top, high)
    factor = 0.25 / math.log(2.0)
    shift = top * factor
    acc = None
    for i in range(pieces):
        weight = jnp.exp2(scores[:, i * size:(i + 1) * size] * factor - shift).astype(BF)
        part = jnp.dot(weight, keys[i * size:(i + 1) * size, :], preferred_element_type=F32)
        acc = part if acc is None else acc + part
    context = acc[:, :LANES] / acc[:, LANES + 1:LANES + 2]
    first = limits[2] + step * block
    position = first + lax.broadcasted_iota(jnp.int32, (block, LANES), 0)
    context = jnp.where(position < limits[0], context, 0.0)
    for s in range(sources):
        low = context[2 * s * half:(2 * s + 1) * half]
        high = context[(2 * s + 1) * half:(2 * s + 2) * half]
        out_ref[s] = merge(swap(low), high).astype(BF)


def attend(limits, queries, keys):
    count = keys.shape[0]
    places, half, _ = queries.shape
    sources = 2
    block = 2 * half * sources
    return pl.pallas_call(
        attend_kernel,
        out_shape=jax.ShapeDtypeStruct(queries.shape, BF),
        grid_spec=pltpu.PrefetchScalarGridSpec(
            num_scalar_prefetch=1,
            grid=(places // sources,),
            in_specs=[
                pl.BlockSpec((sources, half, LANES), lambda i, _: (i, 0, 0)),
                pl.BlockSpec((count, LANES), lambda i, _: (0, 0)),
            ],
            out_specs=pl.BlockSpec((sources, half, LANES), lambda i, _: (i, 0, 0)),
            scratch_shapes=[pltpu.VMEM((count, 2 * LANES), BF), pltpu.VMEM((block, count), F32)],
        ),
        compiler_params=pltpu.CompilerParams(vmem_limit_bytes=VMEM_LIMIT),
        name="attend",
    )(limits, queries, keys)


def output_kernel(
    ctx_ref, w_ref, h_ref, out_ref,
    back, full, part, own, landed, z_out, z_in,
    c_send, c_recv, y_send, y_recv, h_send, h_recv,
):
    seg, x, zl, zh, y = place()
    far = NH - 1 - zh
    total, chunk = h_ref.shape
    half = back.shape[1]
    rows = 2 * half
    batch = total // rows
    heads = w_ref.shape[0] // DH

    partners = [at(seg, x, (zl + k) % NZ, zh, y) for k in range(1, NZ)]
    partners += [at(seg, x, zl, zh, (y + k) % NY) for k in range(1, NY)] + [at(seg, x, zl, far, y)]
    greet(partners)

    def z_copy(k):
        z = (zl + k) % NZ
        return push(ctx_ref.at[z], back.at[zl], c_send.at[k], c_recv.at[zl], at(seg, x, z, zh, y))

    def z_start(k, carry):
        z_copy(k).start()
        return carry

    lax.fori_loop(1, NZ, z_start, 0)
    back[zl] = ctx_ref[zl]

    def z_wait(k, carry):
        z = (zl + NZ - k) % NZ
        push(back.at[z], back.at[z], c_send.at[0], c_recv.at[z], at(seg, x, zl, zh, y)).wait_recv()
        z_copy(k).wait_send()
        return carry

    lax.fori_loop(1, NZ, z_wait, 0)
    for b in range(batch):
        for t in range(heads // 2):
            even = back[b * heads + 2 * t].astype(F32)
            odd = back[b * heads + 2 * t + 1].astype(F32)
            tile = slice(t * LANES, (t + 1) * LANES)
            full[b * rows:b * rows + half, tile] = merge(even, swap(odd)).astype(BF)
            full[b * rows + half:(b + 1) * rows, tile] = merge(swap(even), odd).astype(BF)

    def projected(zz, yy):
        cols = pl.ds(pl.multiple_of((zz * NY + yy) * chunk, chunk), chunk)
        return jnp.dot(full[...], w_ref[:, cols], preferred_element_type=F32)

    def y_copy(k):
        yy = (y + k) % NY
        return push(part.at[yy], landed.at[y], y_send.at[k], y_recv.at[y], at(seg, x, zl, zh, yy))

    def y_start(k, carry):
        yy = (y + k) % NY
        for zz in range(NH):
            part[yy, zz] = projected(zz, yy).astype(BF)
        y_copy(k).start()
        return carry

    lax.fori_loop(1, NY, y_start, 0)
    for zz in range(NH):
        own[zz] = projected(zz, y)

    def y_wait(k, carry):
        yy = (y + NY - k) % NY
        push(landed.at[yy], landed.at[yy], y_send.at[0], y_recv.at[yy], at(seg, x, zl, zh, y)).wait_recv()
        for zz in range(NH):
            own[zz] += landed[yy, zz].astype(F32)
        return carry

    lax.fori_loop(1, NY, y_wait, 0)
    z_out[...] = own[far].astype(BF)
    exchange = push(z_out, z_in, h_send, h_recv, at(seg, x, zl, far, y))
    exchange.start()
    exchange.wait()
    out_ref[...] = (h_ref[...].astype(F32) + own[zh] + z_in[...].astype(F32)).astype(BF)
    for k in range(1, NY):
        y_copy(k).wait_send()


def output(context, w_out, hidden):
    total, chunk = hidden.shape
    places, half, _ = context.shape
    cols = w_out.shape[0]
    dma = pltpu.SemaphoreType.DMA
    vmem = pl.BlockSpec(memory_space=pltpu.VMEM)
    return pl.pallas_call(
        output_kernel,
        out_shape=jax.ShapeDtypeStruct((total, chunk), BF),
        in_specs=[vmem] * 3,
        out_specs=vmem,
        scratch_shapes=[
            pltpu.VMEM((places, half, LANES), BF),
            pltpu.VMEM((total, cols), BF),
            pltpu.VMEM((NY, NH, total, chunk), BF),
            pltpu.VMEM((NH, total, chunk), F32),
            pltpu.VMEM((NY, NH, total, chunk), BF),
            pltpu.VMEM((total, chunk), BF),
            pltpu.VMEM((total, chunk), BF),
            dma((NZ,)),
            dma((NZ,)),
            dma((NY,)),
            dma((NY,)),
            dma(()),
            dma(()),
        ],
        compiler_params=pltpu.CompilerParams(
            collective_id=2, has_side_effects=True, vmem_limit_bytes=VMEM_LIMIT
        ),
        name="output",
    )(context, w_out, hidden)


def body(hidden, memory, w_query, w_key, w_value, w_out, norm_gain, final_gain, lengths):
    seg, x, zl, _, _ = place()
    _, batch, rows, chunk = hidden.shape
    heads = w_query.shape[2] // DH
    own = hidden[0].reshape(batch * rows, chunk)
    mem = memory[0].reshape(batch * rows, chunk)
    gains = jnp.stack([norm_gain[0], jnp.where(seg == 0, norm_gain[0], final_gain)])
    queries, keys = gather(own, mem, w_query[0], w_key[0], w_value[0], gains, rows)
    pair = lax.dynamic_index_in_dim(lengths[0], zl // heads, 0, keepdims=False)
    limits = jnp.concatenate([pair, jnp.array([x * NZ * rows], jnp.int32)])
    context = attend(limits, queries, keys.reshape(NX * NZ * rows, LANES))
    out = output(context, w_out[0], own)
    return out.reshape(1, batch, rows, chunk)


def solution(mesh):
    return jax.shard_map(
        body,
        mesh=mesh,
        in_specs=(
            P("segment", None, "seq", "mp"),
            P("segment", None, "seq", "mp"),
            P("segment", None, "mp"),
            P("segment", None, "mp"),
            P("segment", None, "mp"),
            P("segment", "mp", None),
            P("segment", None),
            P(),
            P("segment", None, None),
        ),
        out_specs=P("segment", None, "seq", "mp"),
        check_vma=False,
    )
```

```python
import math

import jax
import jax.numpy as jnp
from jax import lax
from jax.experimental import pallas as pl
from jax.experimental.pallas import tpu as pltpu
from jax.sharding import PartitionSpec as P

DH = 64
NX, NZ, NH, NY = 4, 8, 2, 4
PIECES = 5
LANES = 128
BF = jnp.bfloat16
F32 = jnp.float32
VMEM_LIMIT = 56 * 1024 * 1024
EARLY, LATE = 0, 1


def place():
    seg, seq, mp = lax.axis_index("segment"), lax.axis_index("seq"), lax.axis_index("mp")
    return seg, seq // NZ, seq % NZ, mp // NY, mp % NY


def at(seg, x, zl, zh, y):
    return (seg, x * NZ + zl, zh * NY + y)


def push(src, dst, send, recv, device):
    return pltpu.make_async_remote_copy(
        src_ref=src, dst_ref=dst, send_sem=send, recv_sem=recv,
        device_id=device, device_id_type=pl.DeviceIdType.MESH,
    )


def greet(partners):
    barrier = pltpu.get_barrier_semaphore()
    for device in partners:
        pl.semaphore_signal(barrier, inc=1, device_id=device, device_id_type=pl.DeviceIdType.MESH)
    pl.semaphore_wait(barrier, len(partners))


def swap(tile):
    return pltpu.roll(tile, DH, 1)


def merge(low, high):
    return jnp.where(lax.broadcasted_iota(jnp.int32, low.shape, 1) < DH, low, high)


def layer_kernel(
    lengths_ref, h_ref, m_ref, wq_hbm, wk_hbm, wv_hbm, wo_hbm, norm_ref, final_ref,
    out_ref,
    hv, wq, wk, wv, wo, gain, xs, accq, acck, accv, ssq, qs, kvs, qa, kva, aux, scores,
    co, back, full, part, own, landed, fs, fin,
    local, z_send, f_send, x_recv, a_send, q_recv, kv_recv, xf_send, c_send, c_recv, y_send, y_recv,
    e_send, e_recv,
):
    seg, x, zl, zh, y = place()
    nc = NZ // 2
    cb, zi = zl // nc, zl % nc
    z4 = (zl + nc) % NZ
    far = NH - 1 - zh
    mp, omp = zh * NY + y, far * NY + y
    batch, rows, chunk = hv.shape
    half = rows // 2
    heads = nc
    width = chunk * NH * NY
    count = NX * NZ * rows
    me = at(seg, x, zl, zh, y)

    loads = [
        pltpu.make_async_copy(src, dst, local.at[i])
        for i, (src, dst) in enumerate(
            [(h_ref, hv), (wq_hbm, wq), (wk_hbm, wk), (wv_hbm, wv), (wo_hbm, wo)]
        )
    ]
    for load in loads:
        load.start()

    partners = [at(seg, x, zl, far, y), at(seg, x, z4, zh, y), at(seg, x, z4, far, y)]
    partners += [at(1 - seg, x, a, b, y) for a, b in [(zl, zh), (zl, far), (z4, zh), (z4, far)]]
    partners += [at(seg, x, zl, zh, (y + k) % NY) for k in range(1, NY)]
    partners += [at(seg, x, cb * nc + (zi + k) % nc, zh, y) for k in range(1, nc)]
    partners += [at(seg, (x + k) % NX, zl, zh, y) for k in range(1, NX)]
    greet(partners)

    def spread(array, src):
        to = array if array else seg
        targets = [
            (EARLY, at(to, x, z4, zh, y)),
            (EARLY, at(to, x, z4, far, y)),
            (LATE, at(to, x, zl, far, y)),
        ]
        if array:
            targets.append((LATE, at(to, x, zl, zh, y)))
        return [
            push(src.at[(cb + 1 - rb) % 2], xs.at[array, rb, mp], z_send.at[array, i], x_recv.at[array, rb, mp], d)
            for i, (rb, d) in enumerate(targets)
        ]

    def arrived(array, rb, c):
        push(xs.at[array, rb, c], xs.at[array, rb, c], f_send.at[0, 0, 0], x_recv.at[array, rb, c], me).wait_recv()

    def along_y(array, rb, c):
        slot = rb * NH + (0 if c is mp else 1)
        return [
            push(xs.at[array, rb, c], xs.at[array, rb, c], f_send.at[array, slot, k], x_recv.at[array, rb, c],
                 at(seg, x, zl, zh, (y + k) % NY))
            for k in range(1, NY)
        ]

    def forward(array, rb, c, wait=True):
        if wait:
            arrived(array, rb, c)
        for copy in along_y(array, rb, c):
            copy.start()

    def both(rb, c):
        forward(0, rb, c)

        @pl.when(seg == 1)
        def _():
            forward(1, rb, c)

    for copy in spread(0, h_ref):
        copy.start()

    @pl.when(seg == 0)
    def _():
        for copy in spread(1, m_ref):
            copy.start()

    loads[0].wait()
    xs[0, LATE, mp] = hv[cb]
    forward(0, LATE, mp, wait=False)

    @pl.when(seg == 1)
    def _():
        forward(1, LATE, mp)

    gain[0:1, :] = norm_ref[...]
    gain[1:2, :] = jnp.where(seg == 0, norm_ref[...], final_ref[...])
    key_length = lengths_ref[cb, 1]

    def fill(i, carry):
        span = pl.ds(pl.multiple_of(i * rows, rows), rows)
        row = i * rows + lax.broadcasted_iota(jnp.int32, (rows, LANES), 0)
        lane = lax.broadcasted_iota(jnp.int32, (rows, LANES), 1)
        bias = jnp.where(row < key_length, 0.0, -1e30)
        aux[span, :] = jnp.where(lane == 0, bias, jnp.where(lane == 1, 1.0, 0.0)).astype(BF)
        return carry

    lax.fori_loop(0, NX * NZ, fill, 0)
    accq[...] = jnp.zeros_like(accq)
    acck[...] = jnp.zeros_like(acck)
    accv[...] = jnp.zeros_like(accv)
    ssq[...] = jnp.zeros_like(ssq)
    for load in loads[1:4]:
        load.wait()

    def squares(values):
        values = values * values
        return sum(values[:, i * LANES:(i + 1) * LANES] for i in range(chunk // LANES))

    def absorb(rb, first, last):
        def step(j, carry):
            c = (zh + j // NY) % NH * NY + (y + j % NY) % NY

            @pl.when(j % NY > 0)
            def _():
                arrived(0, rb, c)

                @pl.when(seg == 1)
                def _():
                    arrived(1, rb, c)

            cols = pl.ds(pl.multiple_of(c * chunk, chunk), chunk)
            xq = xs[0, rb, c].astype(F32)
            ssq[0, rb] += squares(xq)
            accq[rb] += jnp.dot((xq * gain[0:1, cols]).astype(BF), wq[cols, :], preferred_element_type=F32)
            xk = xs[seg, rb, c].astype(F32)
            ssq[1, rb] += squares(xk)
            xk = (xk * gain[1:2, cols]).astype(BF)
            acck[rb] += jnp.dot(xk, wk[cols, :], preferred_element_type=F32)
            accv[rb] += jnp.dot(xk, wv[cols, :], preferred_element_type=F32)
            return carry

        lax.fori_loop(first, last, step, 0)

    zpos = [z4, zl]

    def kv_slot(xx, z):
        return kva.at[pl.ds(pl.multiple_of((xx * NZ + z) * rows, rows), rows)]

    def exchange(rb, k):
        h = (zi + k) % nc
        device = at(seg, x, cb * nc + h, zh, y)
        return (
            push(kvs.at[rb, h], kv_slot(x, zpos[rb]), a_send.at[rb, 0, k], kv_recv.at[x, zpos[rb]], device),
            push(qs.at[rb, h], qa.at[zpos[rb]], a_send.at[rb, 1, k], q_recv.at[zpos[rb]], device),
        )

    def along_x(z, k):
        return push(kv_slot(x, z), kv_slot(x, z), xf_send.at[z, k], kv_recv.at[x, z], at(seg, (x + k) % NX, zl, zh, y))

    def kv_arrived(xx, z):
        push(kv_slot(xx, z), kv_slot(xx, z), xf_send.at[0, 0], kv_recv.at[xx, z], me).wait_recv()

    def project(rb):
        rq = lax.rsqrt(jnp.sum(ssq[0, rb], axis=1, keepdims=True) / width + 1e-06)
        rk = lax.rsqrt(jnp.sum(ssq[1, rb], axis=1, keepdims=True) / width + 1e-06)
        for t in range(heads // 2):
            tile = slice(t * LANES, (t + 1) * LANES)
            k = acck[rb, :, tile] * rk
            v = accv[rb, :, tile] * rk
            q = accq[rb, :, tile] * rq
            kvs[rb, 2 * t] = merge(k, swap(v)).astype(BF)
            kvs[rb, 2 * t + 1] = merge(swap(k), v).astype(BF)
            qs[rb, 2 * t] = merge(q[:half], swap(q[half:])).astype(BF)
            qs[rb, 2 * t + 1] = merge(swap(q[:half]), q[half:]).astype(BF)
        for k in range(1, nc):
            for copy in exchange(rb, k):
                copy.start()
        kva[pl.ds(pl.multiple_of((x * NZ + zpos[rb]) * rows, rows), rows), :] = kvs[rb, zi]
        qa[zpos[rb]] = qs[rb, zi]

    def from_z(rb, k):
        return ((cb + 1 - rb) % 2) * nc + (zi + nc - k) % nc

    def pass_x(rb):
        def step(k, carry):
            z = from_z(rb, k)

            @pl.when(k > 0)
            def _():
                kv_arrived(x, z)

            for i in range(1, NX):
                along_x(z, i).start()
            return carry

        lax.fori_loop(0, nc, step, 0)

    absorb(LATE, 0, NY)
    both(EARLY, mp)
    both(EARLY, omp)
    absorb(EARLY, 0, NH * NY)
    project(EARLY)
    both(LATE, omp)
    pass_x(EARLY)
    absorb(LATE, NY, NH * NY)
    project(LATE)
    pass_x(LATE)

    def collect(rb):
        def step(k, carry):
            z = from_z(rb, k)
            for i in range(1, NX):
                kv_arrived((x + i) % NX, z)

            @pl.when(k > 0)
            def _():
                push(qa.at[z], qa.at[z], a_send.at[0, 0, 0], q_recv.at[z], me).wait_recv()

            return carry

        lax.fori_loop(0, nc, step, 0)

    collect(EARLY)
    collect(LATE)

    sources = 2
    block = sources * rows
    size = count // PIECES
    factor = 0.25 / math.log(2.0)
    query_length = lengths_ref[cb, 0]

    def keys(i):
        span = slice(i * size, (i + 1) * size)
        return jnp.concatenate([kva[span, :], aux[span, :]], axis=1)

    def give_back(z, rb):
        return push(co.at[z], back.at[rb, zi], c_send.at[z], c_recv.at[rb, zi], at(seg, x, cb * nc + z % nc, zh, y))

    def returned(rb, h):
        push(back.at[rb, h], back.at[rb, h], c_send.at[0], c_recv.at[rb, h], me).wait_recv()

    def attend(s, carry):
        turn = s // (nc // 2)
        first = (cb + turn) % 2 * nc + s % (nc // 2) * 2
        rb = 1 - turn
        parts = []
        for e in range(sources):
            packed = qa[first + e].astype(F32)
            parts += [merge(packed, jnp.zeros_like(packed)), merge(swap(packed), jnp.zeros_like(packed))]
        query = jnp.concatenate(parts, axis=0).astype(BF)
        flag = (lax.broadcasted_iota(jnp.int32, (block, LANES), 1) == 0).astype(BF)
        query = jnp.concatenate([query, flag], axis=1)
        top = None
        for i in range(PIECES):
            piece = lax.dot_general(query, keys(i), (((1,), (1,)), ((), ())), preferred_element_type=F32)
            scores[:, i * size:(i + 1) * size] = piece
            high = jnp.max(piece, axis=1, keepdims=True)
            top = high if top is None else jnp.maximum(top, high)
        shift = top * factor
        acc = None
        for i in range(PIECES):
            weight = jnp.exp2(scores[:, i * size:(i + 1) * size] * factor - shift).astype(BF)
            piece = jnp.dot(weight, keys(i), preferred_element_type=F32)
            acc = piece if acc is None else acc + piece
        context = acc[:, :LANES] / acc[:, LANES + 1:LANES + 2]
        position = (x * NZ + first) * rows + lax.broadcasted_iota(jnp.int32, (block, LANES), 0)
        context = jnp.where(position < query_length, context, 0.0)
        for e in range(sources):
            low = context[2 * e * half:(2 * e + 1) * half]
            high = context[(2 * e + 1) * half:(2 * e + 2) * half]
            z = first + e
            co[z] = merge(swap(low), high).astype(BF)

            @pl.when(z % nc != zi)
            def _():
                give_back(z, rb).start()

            @pl.when(z % nc == zi)
            def _():
                back[rb, zi] = co[z]

        @pl.when(s == nc // 2)
        def _():
            multiply(LATE)

        return carry

    def y_copy(rb, k):
        yy = (y + k) % NY
        return push(part.at[rb, yy], landed.at[rb, y], y_send.at[rb, k], y_recv.at[rb, y], at(seg, x, zl, zh, yy))

    def multiply(rb):
        for k in range(1, nc):
            returned(rb, (zi + k) % nc)
        for t in range(heads // 2):
            even = back[rb, 2 * t].astype(F32)
            odd = back[rb, 2 * t + 1].astype(F32)
            tile = slice(t * LANES, (t + 1) * LANES)
            full[:half, tile] = merge(even, swap(odd)).astype(BF)
            full[half:, tile] = merge(swap(even), odd).astype(BF)

        def projected(zz, yy):
            cols = pl.ds(pl.multiple_of((zz * NY + yy) * chunk, chunk), chunk)
            return jnp.dot(full[...], wo[:, cols], preferred_element_type=F32)

        for k in range(1, NY):
            yy = (y + k) % NY
            for zz in range(NH):
                part[rb, yy, zz] = projected(zz, yy).astype(BF)
            y_copy(rb, k).start()
        for zz in range(NH):
            own[rb, zz] = projected(zz, y)

    def add_up(rb):
        for k in range(1, NY):
            yy = (y + NY - k) % NY
            push(landed.at[rb, yy], landed.at[rb, yy], y_send.at[0, 0], y_recv.at[rb, yy], me).wait_recv()
            for zz in range(NH):
                own[rb, zz] += landed[rb, yy, zz].astype(F32)

    def home(i):
        device = [at(seg, x, zl, far, y), at(seg, x, z4, zh, y), at(seg, x, z4, far, y)][i]
        return push(fs.at[i], fin.at[i], e_send.at[i], e_recv.at[i], device)

    loads[4].wait()
    lax.fori_loop(0, nc, attend, 0)
    add_up(LATE)
    fs[0] = own[LATE, far].astype(BF)
    home(0).start()
    multiply(EARLY)
    add_up(EARLY)
    fs[2] = own[EARLY, far].astype(BF)
    home(2).start()
    fs[1] = own[EARLY, zh].astype(BF)
    home(1).start()
    home(0).wait()
    out_ref[cb] = (hv[cb].astype(F32) + own[LATE, zh] + fin[0].astype(F32)).astype(BF)
    home(1).wait()
    home(2).wait()
    out_ref[1 - cb] = (hv[1 - cb].astype(F32) + fin[1].astype(F32) + fin[2].astype(F32)).astype(BF)

    for copy in spread(0, h_ref):
        copy.wait_send()

    @pl.when(seg == 0)
    def _():
        for copy in spread(1, m_ref):
            copy.wait_send()

    for rb in (EARLY, LATE):
        for c in (mp, omp):
            for copy in along_y(0, rb, c):
                copy.wait_send()

            @pl.when(seg == 1)
            def _():
                for copy in along_y(1, rb, c):
                    copy.wait_send()

        for k in range(1, nc):
            for copy in exchange(rb, k):
                copy.wait_send()
        for k in range(1, NY):
            y_copy(rb, k).wait_send()

    def drain(z, carry):
        for k in range(1, NX):
            along_x(z, k).wait_send()

        @pl.when(z % nc != zi)
        def _():
            give_back(z, 0).wait_send()

        return carry

    lax.fori_loop(0, NZ, drain, 0)


def layer(lengths, hidden, memory, w_query, w_key, w_value, w_out, norm_gain, final_gain):
    batch, rows, chunk = hidden.shape
    depth, cols = w_query.shape
    count = NX * NZ * rows
    parts = NH * NY
    nc = NZ // 2
    dma = pltpu.SemaphoreType.DMA
    vmem = pl.BlockSpec(memory_space=pltpu.VMEM)
    hbm = pl.BlockSpec(memory_space=pltpu.HBM)
    smem = pl.BlockSpec(memory_space=pltpu.SMEM)
    return pl.pallas_call(
        layer_kernel,
        out_shape=jax.ShapeDtypeStruct((batch, rows, chunk), BF),
        in_specs=[smem] + [hbm] * 6 + [vmem] * 2,
        out_specs=vmem,
        scratch_shapes=[
            pltpu.VMEM((batch, rows, chunk), BF),
            pltpu.VMEM((depth, cols), BF),
            pltpu.VMEM((depth, cols), BF),
            pltpu.VMEM((depth, cols), BF),
            pltpu.VMEM((cols, depth), BF),
            pltpu.VMEM((2, depth), F32),
            pltpu.VMEM((2, 2, parts, rows, chunk), BF),
            pltpu.VMEM((2, rows, cols), F32),
            pltpu.VMEM((2, rows, cols), F32),
            pltpu.VMEM((2, rows, cols), F32),
            pltpu.VMEM((2, 2, rows, LANES), F32),
            pltpu.VMEM((2, nc, rows // 2, LANES), BF),
            pltpu.VMEM((2, nc, rows, LANES), BF),
            pltpu.VMEM((NZ, rows // 2, LANES), BF),
            pltpu.VMEM((count, LANES), BF),
            pltpu.VMEM((count, LANES), BF),
            pltpu.VMEM((2 * rows, count), F32),
            pltpu.VMEM((NZ, rows // 2, LANES), BF),
            pltpu.VMEM((2, nc, rows // 2, LANES), BF),
            pltpu.VMEM((rows, cols), BF),
            pltpu.VMEM((2, NY, NH, rows, chunk), BF),
            pltpu.VMEM((2, NH, rows, chunk), F32),
            pltpu.VMEM((2, NY, NH, rows, chunk), BF),
            pltpu.VMEM((3, rows, chunk), BF),
            pltpu.VMEM((3, rows, chunk), BF),
            dma((5,)),
            dma((2, 4)),
            dma((2, 4, NY)),
            dma((2, 2, parts)),
            dma((2, 2, nc)),
            dma((NZ,)),
            dma((NX, NZ)),
            dma((NZ, NX)),
            dma((NZ,)),
            dma((2, nc)),
            dma((2, NY)),
            dma((2, NY)),
            dma((3,)),
            dma((3,)),
        ],
        compiler_params=pltpu.CompilerParams(
            collective_id=1, has_side_effects=True, vmem_limit_bytes=VMEM_LIMIT
        ),
        name="layer",
    )(lengths, hidden, memory, w_query, w_key, w_value, w_out, norm_gain, final_gain)


def body(hidden, memory, w_query, w_key, w_value, w_out, norm_gain, final_gain, lengths):
    out = layer(
        lengths[0], hidden[0], memory[0], w_query[0], w_key[0], w_value[0], w_out[0],
        norm_gain, final_gain.reshape(norm_gain.shape),
    )
    return out[None]


def solution(mesh):
    return jax.shard_map(
        body,
        mesh=mesh,
        in_specs=(
            P("segment", None, "seq", "mp"),
            P("segment", None, "seq", "mp"),
            P("segment", None, "mp"),
            P("segment", None, "mp"),
            P("segment", None, "mp"),
            P("segment", "mp", None),
            P("segment", None),
            P(),
            P("segment", None, None),
        ),
        out_specs=P("segment", None, "seq", "mp"),
        check_vma=False,
    )
```

```python
import math

import jax
import jax.numpy as jnp
from jax import lax
from jax.experimental import pallas as pl
from jax.experimental.pallas import tpu as pltpu
from jax.sharding import PartitionSpec as P

DH = 64
NX, NZ, NH, NY = 4, 8, 2, 4
PIECES = 5
LANES = 128
BF = jnp.bfloat16
F32 = jnp.float32
VMEM_LIMIT = 60 * 1024 * 1024
NHF = 2
EARLY, LATE = 0, 1


def place():
    seg, seq, mp = lax.axis_index("segment"), lax.axis_index("seq"), lax.axis_index("mp")
    return seg, seq // NZ, seq % NZ, mp // NY, mp % NY


def at(seg, x, zl, zh, y):
    return (seg, x * NZ + zl, zh * NY + y)


def push(src, dst, send, recv, device):
    return pltpu.make_async_remote_copy(
        src_ref=src, dst_ref=dst, send_sem=send, recv_sem=recv,
        device_id=device, device_id_type=pl.DeviceIdType.MESH,
    )


def swap(tile):
    return pltpu.roll(tile, DH, 1)


def merge(low, high):
    return jnp.where(lax.broadcasted_iota(jnp.int32, low.shape, 1) < DH, low, high)


def layer_kernel(
    lengths_ref, h_ref, m_ref, wq_hbm, wk_hbm, wv_hbm, wo_hbm, norm_ref, final_ref,
    out_ref,
    hv, wq, wk, wv, wo, gain, xs, accq, acck, accv, ssq, qs, kvs, qa, kva, aux, scores, tops, sums,
    co, back, full, part, own, landed, fs, fin,
    local, z_send, f_send, x_recv, a_send, q_recv, kv_recv, xf_send, c_send, c_recv, y_send, y_recv,
    e_send, e_recv,
):
    seg, x, zl, zh, y = place()
    nc = NZ // 2
    cb, zi = zl // nc, zl % nc
    z4 = (zl + nc) % NZ
    far = NH - 1 - zh
    mp, omp = zh * NY + y, far * NY + y
    batch, rows, chunk = hv.shape
    half = rows // 2
    heads = nc
    width = chunk * NH * NY
    group = NX * nc * rows
    me = at(seg, x, zl, zh, y)

    barrier = pltpu.get_barrier_semaphore()
    partners = [at(seg, x, zl, far, y), at(seg, x, z4, zh, y), at(seg, x, z4, far, y)]
    partners += [at(1 - seg, x, a, b, y) for a, b in [(zl, zh), (zl, far), (z4, zh), (z4, far)]]
    partners += [at(seg, x, zl, zh, (y + k) % NY) for k in range(1, NY)]
    partners += [at(seg, x, cb * nc + (zi + k) % nc, zh, y) for k in range(1, nc)]
    partners += [at(seg, (x + k) % NX, zl, zh, y) for k in range(1, NX)]
    for device in partners:
        pl.semaphore_signal(barrier, inc=1, device_id=device, device_id_type=pl.DeviceIdType.MESH)

    loads = [
        pltpu.make_async_copy(src, dst, local.at[i])
        for i, (src, dst) in enumerate(
            [(h_ref, hv), (wq_hbm, wq), (wk_hbm, wk), (wv_hbm, wv), (wo_hbm, wo)]
        )
    ]
    for load in loads:
        load.start()

    pl.semaphore_wait(barrier, len(partners))

    def piece(ref, hf):
        return ref.at[pl.ds(hf * (rows // NHF), rows // NHF)]

    def spread(array, src, rb):
        to = array if array else seg
        if rb == EARLY:
            targets = [at(to, x, z4, zh, y), at(to, x, z4, far, y)]
        else:
            targets = [at(to, x, zl, far, y)]
        return [
            push(piece(src.at[(cb + 1 - rb) % 2], hf), piece(xs.at[array, rb, mp], hf),
                 z_send.at[array, 2 * rb + i, hf], x_recv.at[array, rb, mp, hf], d)
            for hf in range(NHF) for i, d in enumerate(targets)
        ]

    def next_door():
        return [
            push(piece(m_ref.at[cb], hf), piece(xs.at[1, LATE, mp], hf), z_send.at[1, 3, hf],
                 x_recv.at[1, LATE, mp, hf], at(1, x, zl, zh, y))
            for hf in range(NHF)
        ]

    def arrived(array, rb, c, hf):
        spot = piece(xs.at[array, rb, c], hf)
        push(spot, spot, f_send.at[0, 0, 0, 0], x_recv.at[array, rb, c, hf], me).wait_recv()

    def along_y(array, rb, c, hf):
        slot = rb * NH + (0 if c is mp else 1)
        spot = piece(xs.at[array, rb, c], hf)
        return [
            push(spot, spot, f_send.at[array, slot, k, hf], x_recv.at[array, rb, c, hf],
                 at(seg, x, zl, zh, (y + k) % NY))
            for k in range(1, NY)
        ]

    def forward(array, rb, c, hf, wait=True):
        if wait:
            arrived(array, rb, c, hf)
        for copy in along_y(array, rb, c, hf):
            copy.start()

    def both(rb, c, hf):
        forward(0, rb, c, hf)

        @pl.when(seg == 1)
        def _():
            forward(1, rb, c, hf)

    @pl.when(seg == 0)
    def _():
        for copy in next_door() + spread(1, m_ref, EARLY):
            copy.start()

    for copy in spread(0, h_ref, EARLY):
        copy.start()

    @pl.when(seg == 0)
    def _():
        for copy in spread(1, m_ref, LATE):
            copy.start()

    for copy in spread(0, h_ref, LATE):
        copy.start()

    loads[0].wait()
    xs[0, LATE, mp] = hv[cb]
    for hf in range(NHF):
        forward(0, LATE, mp, hf, wait=False)

    @pl.when(seg == 1)
    def _():
        for hf in range(NHF):
            forward(1, LATE, mp, hf)

    key_length = lengths_ref[cb, 1]

    def fill(i, carry):
        span = pl.ds(pl.multiple_of(i * rows, rows), rows)
        first = ((i // nc) % NX * NZ + i // (NX * nc) * nc + i % nc) * rows
        row = first + lax.broadcasted_iota(jnp.int32, (rows, LANES), 0)
        lane = lax.broadcasted_iota(jnp.int32, (rows, LANES), 1)
        bias = jnp.where(row < key_length, 0.0, -1e30)
        aux[span, :] = jnp.where(lane == 0, bias, jnp.where(lane == 1, 1.0, 0.0)).astype(BF)
        return carry

    lax.fori_loop(0, NX * NZ, fill, 0)
    accq[...] = jnp.zeros_like(accq)
    acck[...] = jnp.zeros_like(acck)
    accv[...] = jnp.zeros_like(accv)
    ssq[...] = jnp.zeros_like(ssq)
    gain[0:1, :] = norm_ref[...]
    gain[1:2, :] = jnp.where(seg == 0, norm_ref[...], final_ref[...])
    for load in loads[1:4]:
        load.wait()

    def squares(values):
        values = values * values
        return sum(values[:, i * LANES:(i + 1) * LANES] for i in range(chunk // LANES))

    def absorb(rb, first, last):
        def step(j, carry):
            c = (zh + j // NY) % NH * NY + (y + j % NY) % NY

            @pl.when(j % NY > 0)
            def _():
                for hf in range(NHF):
                    arrived(0, rb, c, hf)

                @pl.when(seg == 1)
                def _():
                    for hf in range(NHF):
                        arrived(1, rb, c, hf)

            cols = pl.ds(pl.multiple_of(c * chunk, chunk), chunk)
            xq = xs[0, rb, c].astype(F32)
            ssq[0, rb] += squares(xq)
            accq[rb] += jnp.dot((xq * gain[0:1, cols]).astype(BF), wq[cols, :], preferred_element_type=F32)
            xk = xs[seg, rb, c].astype(F32)
            ssq[1, rb] += squares(xk)
            xk = (xk * gain[1:2, cols]).astype(BF)
            acck[rb] += jnp.dot(xk, wk[cols, :], preferred_element_type=F32)
            accv[rb] += jnp.dot(xk, wv[cols, :], preferred_element_type=F32)
            return carry

        lax.fori_loop(first, last, step, 0)

    zpos = [z4, zl]

    def kv_slot(xx, z):
        return pl.ds(pl.multiple_of(((z // nc * NX + xx) * nc + z % nc) * rows, rows), rows)

    def exchange(rb, k):
        h = (zi + k) % nc
        device = at(seg, x, cb * nc + h, zh, y)
        z = zpos[rb]
        return (
            push(kvs.at[rb, h], kva.at[kv_slot(x, z)], a_send.at[rb, 0, k], kv_recv.at[x, z], device),
            push(qs.at[rb, h], qa.at[z], a_send.at[rb, 1, k], q_recv.at[z], device),
        )

    def along_x(z, k):
        spot = kva.at[kv_slot(x, z)]
        return push(spot, spot, xf_send.at[z, k], kv_recv.at[x, z], at(seg, (x + k) % NX, zl, zh, y))

    def kv_arrived(xx, z):
        spot = kva.at[kv_slot(xx, z)]
        push(spot, spot, xf_send.at[0, 0], kv_recv.at[xx, z], me).wait_recv()

    def q_arrived(z):
        push(qa.at[z], qa.at[z], a_send.at[0, 0, 0], q_recv.at[z], me).wait_recv()

    def project(rb):
        rq = lax.rsqrt(jnp.sum(ssq[0, rb], axis=1, keepdims=True) / width + 1e-06)
        rk = lax.rsqrt(jnp.sum(ssq[1, rb], axis=1, keepdims=True) / width + 1e-06)
        for t in range(heads // 2):
            tile = slice(t * LANES, (t + 1) * LANES)
            k = acck[rb, :, tile] * rk
            v = accv[rb, :, tile] * rk
            q = accq[rb, :, tile] * rq
            kvs[rb, 2 * t] = merge(k, swap(v)).astype(BF)
            kvs[rb, 2 * t + 1] = merge(swap(k), v).astype(BF)
            qs[rb, 2 * t] = merge(q[:half], swap(q[half:])).astype(BF)
            qs[rb, 2 * t + 1] = merge(swap(q[:half]), q[half:]).astype(BF)
        for k in range(1, nc):
            for copy in exchange(rb, k):
                copy.start()
        kva[kv_slot(x, zpos[rb]), :] = kvs[rb, zi]
        qa[zpos[rb]] = qs[rb, zi]

    def origin(rb):
        return (cb + 1 - rb) % 2 * nc

    def from_z(rb, k):
        return origin(rb) + (zi + nc - k) % nc

    def pass_x(rb, k):
        z = from_z(rb, k)

        @pl.when(k > 0)
        def _():
            kv_arrived(x, z)

        for i in range(1, NX):
            along_x(z, i).start()

    def pass_early(k, carry):
        pass_x(EARLY, k)
        return carry

    def collect(rb):
        def step(k, carry):
            for i in range(1, NX):
                kv_arrived((x + i) % NX, from_z(rb, k))
            return carry

        lax.fori_loop(0, nc, step, 0)

    def collect_queries(rb):
        for k in range(1, nc):
            q_arrived(from_z(rb, k))

    absorb(LATE, 0, 1)
    absorb(LATE, 1, NY)
    for hf in range(NHF):
        both(EARLY, mp, hf)
        both(EARLY, omp, hf)
    absorb(EARLY, 0, NH * NY)
    project(EARLY)
    for hf in range(NHF):
        both(LATE, omp, hf)
    lax.fori_loop(0, nc, pass_early, 0)
    absorb(LATE, NY, NH * NY)
    project(LATE)

    block = nc * half
    size = group // PIECES
    factor = 0.25 / math.log(2.0)
    query_length = lengths_ref[cb, 0]

    def keys(rb, i):
        span = pl.ds(pl.multiple_of((cb + 1 - rb) % 2 * group + i * size, size), size)
        return jnp.concatenate([kva[span, :], aux[span, :]], axis=1)

    def weigh(rb, hf, key_block):
        parts = []
        for i in range(nc):
            packed = qa[origin(rb) + i].astype(F32)
            packed = jnp.where(hf == 0, packed, swap(packed))
            parts.append(merge(packed, jnp.zeros_like(packed)))
        query = jnp.concatenate(parts, axis=0).astype(BF)
        flag = (lax.broadcasted_iota(jnp.int32, (block, LANES), 1) == 0).astype(BF)
        query = jnp.concatenate([query, flag], axis=1)
        top = None
        for i in range(PIECES):
            score = lax.dot_general(query, keys(key_block, i), (((1,), (1,)), ((), ())), preferred_element_type=F32)
            scores[:, i * size:(i + 1) * size] = score
            high = jnp.max(score, axis=1, keepdims=True)
            top = high if top is None else jnp.maximum(top, high)
        top = top * factor
        acc = None
        for i in range(PIECES):
            weight = jnp.exp2(scores[:, i * size:(i + 1) * size] * factor - top).astype(BF)
            some = jnp.dot(weight, keys(key_block, i), preferred_element_type=F32)
            acc = some if acc is None else acc + some
        return top, acc

    def begin(s, carry):
        pass_x(LATE, s)

        @pl.when(s == 0)
        def _():
            collect(EARLY)
            collect_queries(EARLY)

        @pl.when(s == 2)
        def _():
            collect_queries(LATE)

        top, acc = weigh(s // 2, s % 2, EARLY)
        tops[s] = jnp.broadcast_to(top, (block, LANES))
        sums[s] = acc
        return carry

    def give_back(t, i):
        return push(co.at[t, i], back.at[t, zi], c_send.at[t, i], c_recv.at[t, zi], at(seg, x, cb * nc + i, zh, y))

    def complete(t, carry):
        rb, hf = 1 - t // 2, t % 2
        s = rb * 2 + hf
        top, acc = weigh(rb, hf, LATE)
        old = tops[s][:, :1]
        new = jnp.maximum(top, old)
        acc = acc * jnp.exp2(top - new) + sums[s] * jnp.exp2(old - new)
        context = acc[:, :LANES] / acc[:, LANES + 1:LANES + 2]
        for i in range(nc):
            position = (x * NZ + origin(rb) + i) * rows + hf * half
            position = position + lax.broadcasted_iota(jnp.int32, (half, LANES), 0)
            kept = jnp.where(position < query_length, context[i * half:(i + 1) * half], 0.0)
            co[t, i] = kept.astype(BF)

            @pl.when(zi != i)
            def _():
                give_back(t, i).start()

            @pl.when(zi == i)
            def _():
                back[t, zi] = co[t, i]

        @pl.when(t > 0)
        def _():
            multiply(t - 1)

        @pl.when(t > 1)
        def _():
            add_up(t - 2)

        return carry

    def y_copy(t, k):
        yy = (y + k) % NY
        return push(part.at[t, yy], landed.at[t, y], y_send.at[t, k], y_recv.at[t, y], at(seg, x, zl, zh, yy))

    def multiply(t):
        for k in range(1, nc):
            h = (zi + k) % nc
            push(back.at[t, h], back.at[t, h], c_send.at[0, 0], c_recv.at[t, h], me).wait_recv()
        for i in range(heads // 2):
            even = back[t, 2 * i].astype(F32)
            odd = back[t, 2 * i + 1].astype(F32)
            full[:, i * LANES:(i + 1) * LANES] = merge(swap(even), odd).astype(BF)

        def projected(zz, yy):
            cols = pl.ds(pl.multiple_of((zz * NY + yy) * chunk, chunk), chunk)
            return jnp.dot(full[...], wo[:, cols], preferred_element_type=F32)

        for k in range(1, NY):
            yy = (y + k) % NY
            for zz in range(NH):
                part[t, yy, zz] = projected(zz, yy).astype(BF)
            y_copy(t, k).start()
        for zz in range(NH):
            own[t, zz] = projected(zz, y)

    def home(i, hf):
        device = [at(seg, x, zl, far, y), at(seg, x, z4, zh, y), at(seg, x, z4, far, y)][i]
        return push(fs.at[i, hf], fin.at[i, hf], e_send.at[i, hf], e_recv.at[i, hf], device)

    def add_up(t):
        hf = t % 2
        for k in range(1, NY):
            yy = (y + NY - k) % NY
            push(landed.at[t, yy], landed.at[t, yy], y_send.at[0, 0], y_recv.at[t, yy], me).wait_recv()
            for zz in range(NH):
                own[t, zz] += landed[t, yy, zz].astype(F32)

        @pl.when(t < 2)
        def _():
            fs[0, hf] = own[t, far].astype(BF)
            home(0, hf).start()

        @pl.when(t >= 2)
        def _():
            fs[2, hf] = own[t, far].astype(BF)
            home(2, hf).start()
            fs[1, hf] = own[t, zh].astype(BF)
            home(1, hf).start()

    lax.fori_loop(0, 4, begin, 0)
    collect(LATE)
    loads[4].wait()
    lax.fori_loop(0, 4, complete, 0)
    multiply(3)
    add_up(2)
    add_up(3)
    for hf in range(2):
        span = slice(hf * half, (hf + 1) * half)
        home(0, hf).wait()
        out_ref[cb, span] = (hv[cb, span].astype(F32) + own[hf, zh] + fin[0, hf].astype(F32)).astype(BF)
    for hf in range(2):
        span = slice(hf * half, (hf + 1) * half)
        home(1, hf).wait()
        home(2, hf).wait()
        out_ref[1 - cb, span] = (
            hv[1 - cb, span].astype(F32) + fin[1, hf].astype(F32) + fin[2, hf].astype(F32)
        ).astype(BF)

    for copy in spread(0, h_ref, EARLY) + spread(0, h_ref, LATE):
        copy.wait_send()

    @pl.when(seg == 0)
    def _():
        for copy in spread(1, m_ref, EARLY) + spread(1, m_ref, LATE) + next_door():
            copy.wait_send()

    for rb in (EARLY, LATE):
        for c in (mp, omp):
            for hf in range(NHF):
                for copy in along_y(0, rb, c, hf):
                    copy.wait_send()

                @pl.when(seg == 1)
                def _():
                    for copy in along_y(1, rb, c, hf):
                        copy.wait_send()

        for k in range(1, nc):
            for copy in exchange(rb, k):
                copy.wait_send()

    def drain(t, carry):
        for k in range(1, NY):
            y_copy(t, k).wait_send()
        for i in range(nc):
            @pl.when(zi != i)
            def _():
                give_back(t, i).wait_send()

        return carry

    lax.fori_loop(0, 4, drain, 0)

    def drain_x(z, carry):
        for k in range(1, NX):
            along_x(z, k).wait_send()
        return carry

    lax.fori_loop(0, NZ, drain_x, 0)


def layer(lengths, hidden, memory, w_query, w_key, w_value, w_out, norm_gain, final_gain):
    batch, rows, chunk = hidden.shape
    depth, cols = w_query.shape
    count = NX * NZ * rows
    parts = NH * NY
    nc = NZ // 2
    half = rows // 2
    block = nc * half
    dma = pltpu.SemaphoreType.DMA
    vmem = pl.BlockSpec(memory_space=pltpu.VMEM)
    hbm = pl.BlockSpec(memory_space=pltpu.HBM)
    smem = pl.BlockSpec(memory_space=pltpu.SMEM)
    return pl.pallas_call(
        layer_kernel,
        out_shape=jax.ShapeDtypeStruct((batch, rows, chunk), BF),
        in_specs=[smem] + [hbm] * 6 + [vmem] * 2,
        out_specs=vmem,
        scratch_shapes=[
            pltpu.VMEM((batch, rows, chunk), BF),
            pltpu.VMEM((depth, cols), BF),
            pltpu.VMEM((depth, cols), BF),
            pltpu.VMEM((depth, cols), BF),
            pltpu.VMEM((cols, depth), BF),
            pltpu.VMEM((2, depth), F32),
            pltpu.VMEM((2, 2, parts, rows, chunk), BF),
            pltpu.VMEM((2, rows, cols), F32),
            pltpu.VMEM((2, rows, cols), F32),
            pltpu.VMEM((2, rows, cols), F32),
            pltpu.VMEM((2, 2, rows, LANES), F32),
            pltpu.VMEM((2, nc, half, LANES), BF),
            pltpu.VMEM((2, nc, rows, LANES), BF),
            pltpu.VMEM((NZ, half, LANES), BF),
            pltpu.VMEM((count, LANES), BF),
            pltpu.VMEM((count, LANES), BF),
            pltpu.VMEM((block, count // 2), F32),
            pltpu.VMEM((4, block, LANES), F32),
            pltpu.VMEM((4, block, 2 * LANES), F32),
            pltpu.VMEM((4, nc, half, LANES), BF),
            pltpu.VMEM((4, nc, half, LANES), BF),
            pltpu.VMEM((half, cols), BF),
            pltpu.VMEM((4, NY, NH, half, chunk), BF),
            pltpu.VMEM((4, NH, half, chunk), F32),
            pltpu.VMEM((4, NY, NH, half, chunk), BF),
            pltpu.VMEM((3, 2, half, chunk), BF),
            pltpu.VMEM((3, 2, half, chunk), BF),
            dma((5,)),
            dma((2, 4, 2)),
            dma((2, 4, NY, 2)),
            dma((2, 2, parts, 2)),
            dma((2, 2, nc)),
            dma((NZ,)),
            dma((NX, NZ)),
            dma((NZ, NX)),
            dma((4, nc)),
            dma((4, nc)),
            dma((4, NY)),
            dma((4, NY)),
            dma((3, 2)),
            dma((3, 2)),
        ],
        compiler_params=pltpu.CompilerParams(
            collective_id=1, has_side_effects=True, vmem_limit_bytes=VMEM_LIMIT
        ),
        name="layer",
    )(lengths, hidden, memory, w_query, w_key, w_value, w_out, norm_gain, final_gain)


def body(hidden, memory, w_query, w_key, w_value, w_out, norm_gain, final_gain, lengths):
    out = layer(
        lengths[0], hidden[0], memory[0], w_query[0], w_key[0], w_value[0], w_out[0],
        norm_gain, final_gain.reshape(norm_gain.shape),
    )
    return out[None]


def solution(mesh):
    return jax.shard_map(
        body,
        mesh=mesh,
        in_specs=(
            P("segment", None, "seq", "mp"),
            P("segment", None, "seq", "mp"),
            P("segment", None, "mp"),
            P("segment", None, "mp"),
            P("segment", None, "mp"),
            P("segment", "mp", None),
            P("segment", None),
            P(),
            P("segment", None, None),
        ),
        out_specs=P("segment", None, "seq", "mp"),
        check_vma=False,
    )
```

```python
import math

import jax
import jax.numpy as jnp
from jax import lax
from jax.experimental import pallas as pl
from jax.experimental.pallas import tpu as pltpu
from jax.sharding import PartitionSpec as P

DH = 64
NX, NZ, NH, NY = 4, 8, 2, 4
PIECES = 5
LANES = 128
BF = jnp.bfloat16
F32 = jnp.float32
VMEM_LIMIT = 60 * 1024 * 1024
NHF = 2
EARLY, LATE = 0, 1


def place():
    seg, seq, mp = lax.axis_index("segment"), lax.axis_index("seq"), lax.axis_index("mp")
    return seg, seq // NZ, seq % NZ, mp // NY, mp % NY


def at(seg, x, zl, zh, y):
    return (seg, x * NZ + zl, zh * NY + y)


def push(src, dst, send, recv, device):
    return pltpu.make_async_remote_copy(
        src_ref=src, dst_ref=dst, send_sem=send, recv_sem=recv,
        device_id=device, device_id_type=pl.DeviceIdType.MESH,
    )


def swap(tile):
    return pltpu.roll(tile, DH, 1)


def merge(low, high):
    return jnp.where(lax.broadcasted_iota(jnp.int32, low.shape, 1) < DH, low, high)


def layer_kernel(
    lengths_ref, h_ref, m_ref, wq_hbm, wk_hbm, wv_hbm, wo_hbm, norm_ref, final_ref,
    out_ref,
    hv, wq, wk, wv, wo, gain, xs, accq, acck, accv, ssq, qs, kvs, qa, kva, aux, scores, tops, sums,
    co, back, full, part, own, landed, fs, fin,
    local, z_send, f_send, x_recv, a_send, q_recv, kv_recv, xf_send, c_send, c_recv, y_send, y_recv,
    e_send, e_recv,
):
    seg, x, zl, zh, y = place()
    nc = NZ // 2
    cb, zi = zl // nc, zl % nc
    z4 = (zl + nc) % NZ
    far = NH - 1 - zh
    mp, omp = zh * NY + y, far * NY + y
    batch, rows, chunk = hv.shape
    half = rows // 2
    heads = nc
    width = chunk * NH * NY
    group = NX * nc * rows
    me = at(seg, x, zl, zh, y)

    barrier = pltpu.get_barrier_semaphore()
    partners = [at(seg, x, zl, far, y), at(seg, x, z4, zh, y), at(seg, x, z4, far, y)]
    partners += [at(1 - seg, x, a, b, y) for a, b in [(zl, zh), (zl, far), (z4, zh), (z4, far)]]
    partners += [at(seg, x, zl, zh, (y + k) % NY) for k in range(1, NY)]
    partners += [at(seg, x, cb * nc + (zi + k) % nc, zh, y) for k in range(1, nc)]
    partners += [at(seg, (x + k) % NX, zl, zh, y) for k in range(1, NX)]
    for device in partners:
        pl.semaphore_signal(barrier, inc=1, device_id=device, device_id_type=pl.DeviceIdType.MESH)

    loads = [
        pltpu.make_async_copy(src, dst, local.at[i])
        for i, (src, dst) in enumerate(
            [(h_ref, hv), (wq_hbm, wq), (wk_hbm, wk), (wv_hbm, wv), (wo_hbm, wo)]
        )
    ]
    for load in loads:
        load.start()

    pl.semaphore_wait(barrier, len(partners))

    def piece(ref, hf):
        return ref.at[pl.ds(hf * (rows // NHF), rows // NHF)]

    def spread(array, src, rb):
        to = array if array else seg
        if rb == EARLY:
            targets = [at(to, x, z4, zh, y), at(to, x, z4, far, y)]
        else:
            targets = [at(to, x, zl, far, y)]
        return [
            push(piece(src.at[(cb + 1 - rb) % 2], hf), piece(xs.at[array, rb, mp], hf),
                 z_send.at[array, 2 * rb + i, hf], x_recv.at[array, rb, mp, hf], d)
            for hf in range(NHF) for i, d in enumerate(targets)
        ]

    def next_door():
        return [
            push(piece(m_ref.at[cb], hf), piece(xs.at[1, LATE, mp], hf), z_send.at[1, 3, hf],
                 x_recv.at[1, LATE, mp, hf], at(1, x, zl, zh, y))
            for hf in range(NHF)
        ]

    def arrived(array, rb, c, hf):
        spot = piece(xs.at[array, rb, c], hf)
        push(spot, spot, f_send.at[0, 0, 0, 0], x_recv.at[array, rb, c, hf], me).wait_recv()

    def along_y(array, rb, c, hf):
        slot = rb * NH + (0 if c is mp else 1)
        spot = piece(xs.at[array, rb, c], hf)
        return [
            push(spot, spot, f_send.at[array, slot, k, hf], x_recv.at[array, rb, c, hf],
                 at(seg, x, zl, zh, (y + k) % NY))
            for k in range(1, NY)
        ]

    def forward(array, rb, c, hf, wait=True):
        if wait:
            arrived(array, rb, c, hf)
        for copy in along_y(array, rb, c, hf):
            copy.start()

    def both(rb, c, hf):
        forward(0, rb, c, hf)

        @pl.when(seg == 1)
        def _():
            forward(1, rb, c, hf)

    @pl.when(seg == 0)
    def _():
        for copy in next_door() + spread(1, m_ref, EARLY):
            copy.start()

    for copy in spread(0, h_ref, EARLY):
        copy.start()

    @pl.when(seg == 0)
    def _():
        for copy in spread(1, m_ref, LATE):
            copy.start()

    for copy in spread(0, h_ref, LATE):
        copy.start()

    loads[0].wait()
    xs[0, LATE, mp] = hv[cb]
    for hf in range(NHF):
        forward(0, LATE, mp, hf, wait=False)

    @pl.when(seg == 1)
    def _():
        for hf in range(NHF):
            forward(1, LATE, mp, hf)

    key_length = lengths_ref[cb, 1]

    def fill(i, carry):
        span = pl.ds(pl.multiple_of(i * rows, rows), rows)
        first = ((i // nc) % NX * NZ + i // (NX * nc) * nc + i % nc) * rows
        row = first + lax.broadcasted_iota(jnp.int32, (rows, LANES), 0)
        lane = lax.broadcasted_iota(jnp.int32, (rows, LANES), 1)
        bias = jnp.where(row < key_length, 0.0, -1e30)
        aux[span, :] = jnp.where(lane == 0, bias, jnp.where(lane == 1, 1.0, 0.0)).astype(BF)
        return carry

    lax.fori_loop(0, NX * NZ, fill, 0)
    accq[...] = jnp.zeros_like(accq)
    acck[...] = jnp.zeros_like(acck)
    accv[...] = jnp.zeros_like(accv)
    ssq[...] = jnp.zeros_like(ssq)
    gain[0:1, :] = norm_ref[...]
    gain[1:2, :] = jnp.where(seg == 0, norm_ref[...], final_ref[...])
    for load in loads[1:4]:
        load.wait()

    def squares(values):
        values = values * values
        return sum(values[:, i * LANES:(i + 1) * LANES] for i in range(chunk // LANES))

    def absorb(rb, first, last):
        def step(j, carry):
            c = (zh + j // NY) % NH * NY + (y + j % NY) % NY

            @pl.when(j % NY > 0)
            def _():
                for hf in range(NHF):
                    arrived(0, rb, c, hf)

                @pl.when(seg == 1)
                def _():
                    for hf in range(NHF):
                        arrived(1, rb, c, hf)

            cols = pl.ds(pl.multiple_of(c * chunk, chunk), chunk)
            xq = xs[0, rb, c].astype(F32)
            ssq[0, rb] += squares(xq)
            accq[rb] += jnp.dot((xq * gain[0:1, cols]).astype(BF), wq[cols, :], preferred_element_type=F32)
            xk = xs[seg, rb, c].astype(F32)
            ssq[1, rb] += squares(xk)
            xk = (xk * gain[1:2, cols]).astype(BF)
            acck[rb] += jnp.dot(xk, wk[cols, :], preferred_element_type=F32)
            accv[rb] += jnp.dot(xk, wv[cols, :], preferred_element_type=F32)
            return carry

        lax.fori_loop(first, last, step, 0)

    zpos = [z4, zl]

    def kv_slot(xx, z):
        return pl.ds(pl.multiple_of(((z // nc * NX + xx) * nc + z % nc) * rows, rows), rows)

    def exchange(rb, k):
        h = (zi + k) % nc
        device = at(seg, x, cb * nc + h, zh, y)
        z = zpos[rb]
        return (
            push(kvs.at[rb, h], kva.at[kv_slot(x, z)], a_send.at[rb, 0, k], kv_recv.at[x, z], device),
            push(qs.at[rb, h], qa.at[z], a_send.at[rb, 1, k], q_recv.at[z], device),
        )

    def along_x(z, k):
        spot = kva.at[kv_slot(x, z)]
        return push(spot, spot, xf_send.at[z, k], kv_recv.at[x, z], at(seg, (x + k) % NX, zl, zh, y))

    def kv_arrived(xx, z):
        spot = kva.at[kv_slot(xx, z)]
        push(spot, spot, xf_send.at[0, 0], kv_recv.at[xx, z], me).wait_recv()

    def q_arrived(z):
        push(qa.at[z], qa.at[z], a_send.at[0, 0, 0], q_recv.at[z], me).wait_recv()

    def project(rb):
        rq = lax.rsqrt(jnp.sum(ssq[0, rb], axis=1, keepdims=True) / width + 1e-06)
        rk = lax.rsqrt(jnp.sum(ssq[1, rb], axis=1, keepdims=True) / width + 1e-06)
        for t in range(heads // 2):
            tile = slice(t * LANES, (t + 1) * LANES)
            k = acck[rb, :, tile] * rk
            v = accv[rb, :, tile] * rk
            q = accq[rb, :, tile] * rq
            kvs[rb, 2 * t] = merge(k, swap(v)).astype(BF)
            kvs[rb, 2 * t + 1] = merge(swap(k), v).astype(BF)
            qs[rb, 2 * t] = merge(q[:half], swap(q[half:])).astype(BF)
            qs[rb, 2 * t + 1] = merge(swap(q[:half]), q[half:]).astype(BF)
        for k in range(1, nc):
            for copy in exchange(rb, k):
                copy.start()
        kva[kv_slot(x, zpos[rb]), :] = kvs[rb, zi]
        qa[zpos[rb]] = qs[rb, zi]

    def origin(rb):
        return (cb + 1 - rb) % 2 * nc

    def from_z(rb, k):
        return origin(rb) + (zi + nc - k) % nc

    def pass_x(rb, k):
        z = from_z(rb, k)

        @pl.when(k > 0)
        def _():
            kv_arrived(x, z)

        for i in range(1, NX):
            along_x(z, i).start()

    def pass_early(k, carry):
        pass_x(EARLY, k)
        return carry

    def collect(rb):
        def step(k, carry):
            for i in range(1, NX):
                kv_arrived((x + i) % NX, from_z(rb, k))
            return carry

        lax.fori_loop(0, nc, step, 0)

    def collect_queries(rb):
        for k in range(1, nc):
            q_arrived(from_z(rb, k))

    absorb(LATE, 0, 1)
    absorb(LATE, 1, NY)
    for hf in range(NHF):
        both(EARLY, mp, hf)
        both(EARLY, omp, hf)
    absorb(EARLY, 0, NH * NY)
    project(EARLY)
    for hf in range(NHF):
        both(LATE, omp, hf)
    lax.fori_loop(0, nc, pass_early, 0)
    absorb(LATE, NY, NH * NY)
    project(LATE)

    block = nc * half
    size = group // PIECES
    factor = 0.25 / math.log(2.0)
    query_length = lengths_ref[cb, 0]

    def keys(rb, i):
        span = pl.ds(pl.multiple_of((cb + 1 - rb) % 2 * group + i * size, size), size)
        return jnp.concatenate([kva[span, :], aux[span, :]], axis=1)

    def weigh(rb, hf, key_block):
        parts = []
        for i in range(nc):
            packed = qa[origin(rb) + i].astype(F32)
            packed = jnp.where(hf == 0, packed, swap(packed))
            parts.append(merge(packed, jnp.zeros_like(packed)))
        query = jnp.concatenate(parts, axis=0).astype(BF)
        flag = (lax.broadcasted_iota(jnp.int32, (block, LANES), 1) == 0).astype(BF)
        query = jnp.concatenate([query, flag], axis=1)
        top = None
        for i in range(PIECES):
            score = lax.dot_general(query, keys(key_block, i), (((1,), (1,)), ((), ())), preferred_element_type=F32)
            scores[:, i * size:(i + 1) * size] = score
            high = jnp.max(score, axis=1, keepdims=True)
            top = high if top is None else jnp.maximum(top, high)
        top = top * factor
        acc = None
        for i in range(PIECES):
            weight = jnp.exp2(scores[:, i * size:(i + 1) * size] * factor - top).astype(BF)
            some = jnp.dot(weight, keys(key_block, i), preferred_element_type=F32)
            acc = some if acc is None else acc + some
        return top, acc

    def begin(s, carry):
        pass_x(LATE, s)

        @pl.when(s == 0)
        def _():
            collect(EARLY)
            collect_queries(EARLY)

        @pl.when(s == 2)
        def _():
            collect_queries(LATE)

        top, acc = weigh(s // 2, s % 2, EARLY)
        tops[s] = jnp.broadcast_to(top, (block, LANES))
        sums[s] = acc
        return carry

    def give_back(t, i):
        return push(co.at[t, i], back.at[t, zi], c_send.at[t, i], c_recv.at[t, zi], at(seg, x, cb * nc + i, zh, y))

    def complete(t, carry):
        rb, hf = 1 - t // 2, t % 2
        s = rb * 2 + hf
        top, acc = weigh(rb, hf, LATE)
        old = tops[s][:, :1]
        new = jnp.maximum(top, old)
        acc = acc * jnp.exp2(top - new) + sums[s] * jnp.exp2(old - new)
        context = acc[:, :LANES] / acc[:, LANES + 1:LANES + 2]
        for i in range(nc):
            position = (x * NZ + origin(rb) + i) * rows + hf * half
            position = position + lax.broadcasted_iota(jnp.int32, (half, LANES), 0)
            kept = jnp.where(position < query_length, context[i * half:(i + 1) * half], 0.0)
            co[t, i] = kept.astype(BF)

            @pl.when(zi != i)
            def _():
                give_back(t, i).start()

            @pl.when(zi == i)
            def _():
                back[t, zi] = co[t, i]

        @pl.when(t > 1)
        def _():
            multiply(t - 2)

        return carry

    def y_copy(t, k):
        yy = (y + k) % NY
        return push(part.at[t, yy], landed.at[t, y], y_send.at[t, k], y_recv.at[t, y], at(seg, x, zl, zh, yy))

    def multiply(t):
        for k in range(1, nc):
            h = (zi + k) % nc
            push(back.at[t, h], back.at[t, h], c_send.at[0, 0], c_recv.at[t, h], me).wait_recv()
        for i in range(heads // 2):
            even = back[t, 2 * i].astype(F32)
            odd = back[t, 2 * i + 1].astype(F32)
            full[:, i * LANES:(i + 1) * LANES] = merge(swap(even), odd).astype(BF)

        def projected(zz, yy):
            cols = pl.ds(pl.multiple_of((zz * NY + yy) * chunk, chunk), chunk)
            return jnp.dot(full[...], wo[:, cols], preferred_element_type=F32)

        for k in range(1, NY):
            yy = (y + k) % NY
            for zz in range(NH):
                part[t, yy, zz] = projected(zz, yy).astype(BF)
            y_copy(t, k).start()
        for zz in range(NH):
            own[t, zz] = projected(zz, y)

    def home(i, hf):
        device = [at(seg, x, zl, far, y), at(seg, x, z4, zh, y), at(seg, x, z4, far, y)][i]
        return push(fs.at[i, hf], fin.at[i, hf], e_send.at[i, hf], e_recv.at[i, hf], device)

    def add_up(t):
        hf = t % 2
        for k in range(1, NY):
            yy = (y + NY - k) % NY
            push(landed.at[t, yy], landed.at[t, yy], y_send.at[0, 0], y_recv.at[t, yy], me).wait_recv()
            for zz in range(NH):
                own[t, zz] += landed[t, yy, zz].astype(F32)

        @pl.when(t < 2)
        def _():
            fs[0, hf] = own[t, far].astype(BF)
            home(0, hf).start()

        @pl.when(t >= 2)
        def _():
            fs[2, hf] = own[t, far].astype(BF)
            home(2, hf).start()
            fs[1, hf] = own[t, zh].astype(BF)
            home(1, hf).start()

    lax.fori_loop(0, 4, begin, 0)
    collect(LATE)
    loads[4].wait()
    lax.fori_loop(0, 4, complete, 0)
    add_up(0)
    multiply(2)
    add_up(1)
    multiply(3)
    add_up(2)
    add_up(3)
    for hf in range(2):
        span = slice(hf * half, (hf + 1) * half)
        home(0, hf).wait()
        out_ref[cb, span] = (hv[cb, span].astype(F32) + own[hf, zh] + fin[0, hf].astype(F32)).astype(BF)
    for hf in range(2):
        span = slice(hf * half, (hf + 1) * half)
        home(1, hf).wait()
        home(2, hf).wait()
        out_ref[1 - cb, span] = (
            hv[1 - cb, span].astype(F32) + fin[1, hf].astype(F32) + fin[2, hf].astype(F32)
        ).astype(BF)

    for copy in spread(0, h_ref, EARLY) + spread(0, h_ref, LATE):
        copy.wait_send()

    @pl.when(seg == 0)
    def _():
        for copy in spread(1, m_ref, EARLY) + spread(1, m_ref, LATE) + next_door():
            copy.wait_send()

    for rb in (EARLY, LATE):
        for c in (mp, omp):
            for hf in range(NHF):
                for copy in along_y(0, rb, c, hf):
                    copy.wait_send()

                @pl.when(seg == 1)
                def _():
                    for copy in along_y(1, rb, c, hf):
                        copy.wait_send()

        for k in range(1, nc):
            for copy in exchange(rb, k):
                copy.wait_send()

    def drain(t, carry):
        for k in range(1, NY):
            y_copy(t, k).wait_send()
        for i in range(nc):
            @pl.when(zi != i)
            def _():
                give_back(t, i).wait_send()

        return carry

    lax.fori_loop(0, 4, drain, 0)

    def drain_x(z, carry):
        for k in range(1, NX):
            along_x(z, k).wait_send()
        return carry

    lax.fori_loop(0, NZ, drain_x, 0)


def layer(lengths, hidden, memory, w_query, w_key, w_value, w_out, norm_gain, final_gain):
    batch, rows, chunk = hidden.shape
    depth, cols = w_query.shape
    count = NX * NZ * rows
    parts = NH * NY
    nc = NZ // 2
    half = rows // 2
    block = nc * half
    dma = pltpu.SemaphoreType.DMA
    vmem = pl.BlockSpec(memory_space=pltpu.VMEM)
    hbm = pl.BlockSpec(memory_space=pltpu.HBM)
    smem = pl.BlockSpec(memory_space=pltpu.SMEM)
    return pl.pallas_call(
        layer_kernel,
        out_shape=jax.ShapeDtypeStruct((batch, rows, chunk), BF),
        in_specs=[smem] + [hbm] * 6 + [vmem] * 2,
        out_specs=vmem,
        scratch_shapes=[
            pltpu.VMEM((batch, rows, chunk), BF),
            pltpu.VMEM((depth, cols), BF),
            pltpu.VMEM((depth, cols), BF),
            pltpu.VMEM((depth, cols), BF),
            pltpu.VMEM((cols, depth), BF),
            pltpu.VMEM((2, depth), F32),
            pltpu.VMEM((2, 2, parts, rows, chunk), BF),
            pltpu.VMEM((2, rows, cols), F32),
            pltpu.VMEM((2, rows, cols), F32),
            pltpu.VMEM((2, rows, cols), F32),
            pltpu.VMEM((2, 2, rows, LANES), F32),
            pltpu.VMEM((2, nc, half, LANES), BF),
            pltpu.VMEM((2, nc, rows, LANES), BF),
            pltpu.VMEM((NZ, half, LANES), BF),
            pltpu.VMEM((count, LANES), BF),
            pltpu.VMEM((count, LANES), BF),
            pltpu.VMEM((block, count // 2), F32),
            pltpu.VMEM((4, block, LANES), F32),
            pltpu.VMEM((4, block, 2 * LANES), F32),
            pltpu.VMEM((4, nc, half, LANES), BF),
            pltpu.VMEM((4, nc, half, LANES), BF),
            pltpu.VMEM((half, cols), BF),
            pltpu.VMEM((4, NY, NH, half, chunk), BF),
            pltpu.VMEM((4, NH, half, chunk), F32),
            pltpu.VMEM((4, NY, NH, half, chunk), BF),
            pltpu.VMEM((3, 2, half, chunk), BF),
            pltpu.VMEM((3, 2, half, chunk), BF),
            dma((5,)),
            dma((2, 4, 2)),
            dma((2, 4, NY, 2)),
            dma((2, 2, parts, 2)),
            dma((2, 2, nc)),
            dma((NZ,)),
            dma((NX, NZ)),
            dma((NZ, NX)),
            dma((4, nc)),
            dma((4, nc)),
            dma((4, NY)),
            dma((4, NY)),
            dma((3, 2)),
            dma((3, 2)),
        ],
        compiler_params=pltpu.CompilerParams(
            collective_id=1, has_side_effects=True, vmem_limit_bytes=VMEM_LIMIT
        ),
        name="layer",
    )(lengths, hidden, memory, w_query, w_key, w_value, w_out, norm_gain, final_gain)


def body(hidden, memory, w_query, w_key, w_value, w_out, norm_gain, final_gain, lengths):
    out = layer(
        lengths[0], hidden[0], memory[0], w_query[0], w_key[0], w_value[0], w_out[0],
        norm_gain, final_gain.reshape(norm_gain.shape),
    )
    return out[None]


def solution(mesh):
    return jax.shard_map(
        body,
        mesh=mesh,
        in_specs=(
            P("segment", None, "seq", "mp"),
            P("segment", None, "seq", "mp"),
            P("segment", None, "mp"),
            P("segment", None, "mp"),
            P("segment", None, "mp"),
            P("segment", "mp", None),
            P("segment", None),
            P(),
            P("segment", None, None),
        ),
        out_specs=P("segment", None, "seq", "mp"),
        check_vma=False,
    )
```

```python
import math

import jax
import jax.numpy as jnp
from jax import lax
from jax.experimental import pallas as pl
from jax.experimental.pallas import tpu as pltpu
from jax.sharding import PartitionSpec as P

DH = 64
NX, NZ, NH, NY = 4, 8, 2, 4
PIECES = 5
LANES = 128
BF = jnp.bfloat16
F32 = jnp.float32
VMEM_LIMIT = 60 * 1024 * 1024
NHF = 2
EARLY, LATE = 0, 1


def place():
    seg, seq, mp = lax.axis_index("segment"), lax.axis_index("seq"), lax.axis_index("mp")
    return seg, seq // NZ, seq % NZ, mp // NY, mp % NY


def at(seg, x, zl, zh, y):
    return (seg, x * NZ + zl, zh * NY + y)


def push(src, dst, send, recv, device):
    return pltpu.make_async_remote_copy(
        src_ref=src, dst_ref=dst, send_sem=send, recv_sem=recv,
        device_id=device, device_id_type=pl.DeviceIdType.MESH,
    )


def swap(tile):
    return pltpu.roll(tile, DH, 1)


def merge(low, high):
    return jnp.where(lax.broadcasted_iota(jnp.int32, low.shape, 1) < DH, low, high)


def layer_kernel(
    lengths_ref, h_ref, m_ref, wq_hbm, wk_hbm, wv_hbm, wo_hbm, norm_ref, final_ref,
    out_ref,
    hv, wq, wk, wv, wo, gain, xs, accq, acck, accv, ssq, qs, kvs, qa, kva, aux, scores, tops, sums,
    co, back, full, part, own, landed, fs, fin,
    local, z_send, f_send, x_recv, a_send, q_recv, kv_recv, xf_send, c_send, c_recv, y_send, y_recv,
    e_send, e_recv,
):
    seg, x, zl, zh, y = place()
    nc = NZ // 2
    cb, zi = zl // nc, zl % nc
    z4 = (zl + nc) % NZ
    far = NH - 1 - zh
    mp, omp = zh * NY + y, far * NY + y
    batch, rows, chunk = hv.shape
    half = rows // 2
    heads = nc
    width = chunk * NH * NY
    group = NX * nc * rows
    me = at(seg, x, zl, zh, y)

    barrier = pltpu.get_barrier_semaphore()
    partners = [at(seg, x, zl, far, y), at(seg, x, z4, zh, y), at(seg, x, z4, far, y)]
    partners += [at(1 - seg, x, a, b, y) for a, b in [(zl, zh), (zl, far), (z4, zh), (z4, far)]]
    partners += [at(seg, x, zl, zh, (y + k) % NY) for k in range(1, NY)]
    partners += [at(seg, x, cb * nc + (zi + k) % nc, zh, y) for k in range(1, nc)]
    partners += [at(seg, (x + k) % NX, zl, zh, y) for k in range(1, NX)]
    for device in partners:
        pl.semaphore_signal(barrier, inc=1, device_id=device, device_id_type=pl.DeviceIdType.MESH)

    loads = [
        pltpu.make_async_copy(src, dst, local.at[i])
        for i, (src, dst) in enumerate(
            [(h_ref, hv), (wq_hbm, wq), (wk_hbm, wk), (wv_hbm, wv), (wo_hbm, wo)]
        )
    ]
    for load in loads:
        load.start()

    pl.semaphore_wait(barrier, len(partners))

    def piece(ref, hf):
        return ref.at[pl.ds(hf * (rows // NHF), rows // NHF)]

    def spread(array, src, rb):
        to = array if array else seg
        if rb == EARLY:
            targets = [at(to, x, z4, zh, y), at(to, x, z4, far, y)]
        else:
            targets = [at(to, x, zl, far, y)]
        return [
            push(piece(src.at[(cb + 1 - rb) % 2], hf), piece(xs.at[array, rb, mp], hf),
                 z_send.at[array, 2 * rb + i, hf], x_recv.at[array, rb, mp, hf], d)
            for hf in range(NHF) for i, d in enumerate(targets)
        ]

    def next_door():
        return [
            push(piece(m_ref.at[cb], hf), piece(xs.at[1, LATE, mp], hf), z_send.at[1, 3, hf],
                 x_recv.at[1, LATE, mp, hf], at(1, x, zl, zh, y))
            for hf in range(NHF)
        ]

    def arrived(array, rb, c, hf):
        spot = piece(xs.at[array, rb, c], hf)
        push(spot, spot, f_send.at[0, 0, 0, 0], x_recv.at[array, rb, c, hf], me).wait_recv()

    def along_y(array, rb, c, hf):
        slot = rb * NH + (0 if c is mp else 1)
        spot = piece(xs.at[array, rb, c], hf)
        return [
            push(spot, spot, f_send.at[array, slot, k, hf], x_recv.at[array, rb, c, hf],
                 at(seg, x, zl, zh, (y + k) % NY))
            for k in (2, 1, 3)
        ]

    def forward(array, rb, c, hf, wait=True):
        if wait:
            arrived(array, rb, c, hf)
        for copy in along_y(array, rb, c, hf):
            copy.start()

    def both(rb, c, hf):
        forward(0, rb, c, hf)

        @pl.when(seg == 1)
        def _():
            forward(1, rb, c, hf)

    @pl.when(seg == 0)
    def _():
        for copy in next_door() + spread(1, m_ref, EARLY):
            copy.start()

    for copy in spread(0, h_ref, EARLY):
        copy.start()

    @pl.when(seg == 0)
    def _():
        for copy in spread(1, m_ref, LATE):
            copy.start()

    for copy in spread(0, h_ref, LATE):
        copy.start()

    loads[0].wait()
    xs[0, LATE, mp] = hv[cb]
    for hf in range(NHF):
        forward(0, LATE, mp, hf, wait=False)

    @pl.when(seg == 1)
    def _():
        for hf in range(NHF):
            forward(1, LATE, mp, hf)

    key_length = lengths_ref[cb, 1]

    def fill(i, carry):
        span = pl.ds(pl.multiple_of(i * rows, rows), rows)
        first = ((i // nc) % NX * NZ + i // (NX * nc) * nc + i % nc) * rows
        row = first + lax.broadcasted_iota(jnp.int32, (rows, LANES), 0)
        lane = lax.broadcasted_iota(jnp.int32, (rows, LANES), 1)
        bias = jnp.where(row < key_length, 0.0, -1e30)
        aux[span, :] = jnp.where(lane == 0, bias, jnp.where(lane == 1, 1.0, 0.0)).astype(BF)
        return carry

    lax.fori_loop(0, NX * NZ, fill, 0)
    accq[...] = jnp.zeros_like(accq)
    acck[...] = jnp.zeros_like(acck)
    accv[...] = jnp.zeros_like(accv)
    ssq[...] = jnp.zeros_like(ssq)
    gain[0:1, :] = norm_ref[...]
    gain[1:2, :] = jnp.where(seg == 0, norm_ref[...], final_ref[...])
    for load in loads[1:4]:
        load.wait()

    def squares(values):
        values = values * values
        return sum(values[:, i * LANES:(i + 1) * LANES] for i in range(chunk // LANES))

    def absorb(rb, first, last):
        def step(j, carry):
            c = (zh + j // NY) % NH * NY + (y + j % NY) % NY

            @pl.when(j % NY > 0)
            def _():
                for hf in range(NHF):
                    arrived(0, rb, c, hf)

                @pl.when(seg == 1)
                def _():
                    for hf in range(NHF):
                        arrived(1, rb, c, hf)

            cols = pl.ds(pl.multiple_of(c * chunk, chunk), chunk)
            xq = xs[0, rb, c].astype(F32)
            ssq[0, rb] += squares(xq)
            accq[rb] += jnp.dot((xq * gain[0:1, cols]).astype(BF), wq[cols, :], preferred_element_type=F32)
            xk = xs[seg, rb, c].astype(F32)
            ssq[1, rb] += squares(xk)
            xk = (xk * gain[1:2, cols]).astype(BF)
            acck[rb] += jnp.dot(xk, wk[cols, :], preferred_element_type=F32)
            accv[rb] += jnp.dot(xk, wv[cols, :], preferred_element_type=F32)
            return carry

        lax.fori_loop(first, last, step, 0)

    zpos = [z4, zl]

    def kv_slot(xx, z):
        return pl.ds(pl.multiple_of(((z // nc * NX + xx) * nc + z % nc) * rows, rows), rows)

    def exchange(rb, k):
        h = (zi + k) % nc
        device = at(seg, x, cb * nc + h, zh, y)
        z = zpos[rb]
        return (
            push(kvs.at[rb, h], kva.at[kv_slot(x, z)], a_send.at[rb, 0, k], kv_recv.at[x, z], device),
            push(qs.at[rb, h], qa.at[z], a_send.at[rb, 1, k], q_recv.at[z], device),
        )

    def along_x(z, k):
        spot = kva.at[kv_slot(x, z)]
        return push(spot, spot, xf_send.at[z, k], kv_recv.at[x, z], at(seg, (x + k) % NX, zl, zh, y))

    def kv_arrived(xx, z):
        spot = kva.at[kv_slot(xx, z)]
        push(spot, spot, xf_send.at[0, 0], kv_recv.at[xx, z], me).wait_recv()

    def q_arrived(z):
        push(qa.at[z], qa.at[z], a_send.at[0, 0, 0], q_recv.at[z], me).wait_recv()

    def project(rb):
        rq = lax.rsqrt(jnp.sum(ssq[0, rb], axis=1, keepdims=True) / width + 1e-06)
        rk = lax.rsqrt(jnp.sum(ssq[1, rb], axis=1, keepdims=True) / width + 1e-06)
        for t in range(heads // 2):
            tile = slice(t * LANES, (t + 1) * LANES)
            k = acck[rb, :, tile] * rk
            v = accv[rb, :, tile] * rk
            q = accq[rb, :, tile] * rq
            kvs[rb, 2 * t] = merge(k, swap(v)).astype(BF)
            kvs[rb, 2 * t + 1] = merge(swap(k), v).astype(BF)
            qs[rb, 2 * t] = merge(q[:half], swap(q[half:])).astype(BF)
            qs[rb, 2 * t + 1] = merge(swap(q[:half]), q[half:]).astype(BF)
        for k in range(1, nc):
            for copy in exchange(rb, k):
                copy.start()
        kva[kv_slot(x, zpos[rb]), :] = kvs[rb, zi]
        qa[zpos[rb]] = qs[rb, zi]

    def origin(rb):
        return (cb + 1 - rb) % 2 * nc

    def from_z(rb, k):
        return origin(rb) + (zi + nc - k) % nc

    def pass_x(rb, k):
        z = from_z(rb, k)

        @pl.when(k > 0)
        def _():
            kv_arrived(x, z)

        for i in range(1, NX):
            along_x(z, i).start()

    def pass_early(k, carry):
        pass_x(EARLY, k)
        return carry

    def collect(rb):
        def step(k, carry):
            for i in range(1, NX):
                kv_arrived((x + i) % NX, from_z(rb, k))
            return carry

        lax.fori_loop(0, nc, step, 0)

    def collect_queries(rb):
        for k in range(1, nc):
            q_arrived(from_z(rb, k))

    absorb(LATE, 0, 1)
    absorb(LATE, 1, NY)
    for hf in range(NHF):
        both(EARLY, mp, hf)
        both(EARLY, omp, hf)
    absorb(EARLY, 0, NH * NY)
    project(EARLY)
    for hf in range(NHF):
        both(LATE, omp, hf)
    lax.fori_loop(0, nc, pass_early, 0)
    absorb(LATE, NY, NH * NY)
    project(LATE)

    block = nc * half
    size = group // PIECES
    factor = 0.25 / math.log(2.0)
    query_length = lengths_ref[cb, 0]

    def keys(rb, i):
        span = pl.ds(pl.multiple_of((cb + 1 - rb) % 2 * group + i * size, size), size)
        return jnp.concatenate([kva[span, :], aux[span, :]], axis=1)

    def weigh(rb, hf, key_block):
        parts = []
        for i in range(nc):
            packed = qa[origin(rb) + i].astype(F32)
            packed = jnp.where(hf == 0, packed, swap(packed))
            parts.append(merge(packed, jnp.zeros_like(packed)))
        query = jnp.concatenate(parts, axis=0).astype(BF)
        flag = (lax.broadcasted_iota(jnp.int32, (block, LANES), 1) == 0).astype(BF)
        query = jnp.concatenate([query, flag], axis=1)
        top = None
        for i in range(PIECES):
            score = lax.dot_general(query, keys(key_block, i), (((1,), (1,)), ((), ())), preferred_element_type=F32)
            scores[:, i * size:(i + 1) * size] = score
            high = jnp.max(score, axis=1, keepdims=True)
            top = high if top is None else jnp.maximum(top, high)
        top = top * factor
        acc = None
        for i in range(PIECES):
            weight = jnp.exp2(scores[:, i * size:(i + 1) * size] * factor - top).astype(BF)
            some = jnp.dot(weight, keys(key_block, i), preferred_element_type=F32)
            acc = some if acc is None else acc + some
        return top, acc

    def begin(s, carry):
        pass_x(LATE, s)

        @pl.when(s == 0)
        def _():
            collect(EARLY)
            collect_queries(EARLY)

        @pl.when(s == 2)
        def _():
            collect_queries(LATE)

        top, acc = weigh(s // 2, s % 2, EARLY)
        tops[s] = jnp.broadcast_to(top, (block, LANES))
        sums[s] = acc
        return carry

    def give_back(t, i):
        return push(co.at[t, i], back.at[t, zi], c_send.at[t, i], c_recv.at[t, zi], at(seg, x, cb * nc + i, zh, y))

    def complete(t, carry):
        rb, hf = 1 - t // 2, t % 2
        s = rb * 2 + hf
        top, acc = weigh(rb, hf, LATE)
        old = tops[s][:, :1]
        new = jnp.maximum(top, old)
        acc = acc * jnp.exp2(top - new) + sums[s] * jnp.exp2(old - new)
        context = acc[:, :LANES] / acc[:, LANES + 1:LANES + 2]
        for i in range(nc):
            position = (x * NZ + origin(rb) + i) * rows + hf * half
            position = position + lax.broadcasted_iota(jnp.int32, (half, LANES), 0)
            kept = jnp.where(position < query_length, context[i * half:(i + 1) * half], 0.0)
            co[t, i] = kept.astype(BF)

            @pl.when(zi != i)
            def _():
                give_back(t, i).start()

            @pl.when(zi == i)
            def _():
                back[t, zi] = co[t, i]

        @pl.when(t > 1)
        def _():
            multiply(t - 2)

        return carry

    def y_copy(t, k):
        yy = (y + k) % NY
        return push(part.at[t, yy], landed.at[t, y], y_send.at[t, k], y_recv.at[t, y], at(seg, x, zl, zh, yy))

    def multiply(t):
        for k in range(1, nc):
            h = (zi + k) % nc
            push(back.at[t, h], back.at[t, h], c_send.at[0, 0], c_recv.at[t, h], me).wait_recv()
        for i in range(heads // 2):
            even = back[t, 2 * i].astype(F32)
            odd = back[t, 2 * i + 1].astype(F32)
            full[:, i * LANES:(i + 1) * LANES] = merge(swap(even), odd).astype(BF)

        def projected(zz, yy):
            cols = pl.ds(pl.multiple_of((zz * NY + yy) * chunk, chunk), chunk)
            return jnp.dot(full[...], wo[:, cols], preferred_element_type=F32)

        for k in (2, 1, 3):
            yy = (y + k) % NY
            for zz in range(NH):
                part[t, yy, zz] = projected(zz, yy).astype(BF)
            y_copy(t, k).start()
        for zz in range(NH):
            own[t, zz] = projected(zz, y)

    def home(i, hf):
        device = [at(seg, x, zl, far, y), at(seg, x, z4, zh, y), at(seg, x, z4, far, y)][i]
        return push(fs.at[i, hf], fin.at[i, hf], e_send.at[i, hf], e_recv.at[i, hf], device)

    def add_up(t):
        hf = t % 2
        for k in range(1, NY):
            yy = (y + NY - k) % NY
            push(landed.at[t, yy], landed.at[t, yy], y_send.at[0, 0], y_recv.at[t, yy], me).wait_recv()
            for zz in range(NH):
                own[t, zz] += landed[t, yy, zz].astype(F32)

        @pl.when(t < 2)
        def _():
            fs[0, hf] = own[t, far].astype(BF)
            home(0, hf).start()

        @pl.when(t >= 2)
        def _():
            fs[2, hf] = own[t, far].astype(BF)
            home(2, hf).start()
            fs[1, hf] = own[t, zh].astype(BF)
            home(1, hf).start()

    lax.fori_loop(0, 4, begin, 0)
    collect(LATE)
    loads[4].wait()
    lax.fori_loop(0, 4, complete, 0)
    add_up(0)
    multiply(2)
    add_up(1)
    multiply(3)
    add_up(2)
    add_up(3)
    for hf in range(2):
        span = slice(hf * half, (hf + 1) * half)
        home(0, hf).wait()
        out_ref[cb, span] = (hv[cb, span].astype(F32) + own[hf, zh] + fin[0, hf].astype(F32)).astype(BF)
    for hf in range(2):
        span = slice(hf * half, (hf + 1) * half)
        home(1, hf).wait()
        home(2, hf).wait()
        out_ref[1 - cb, span] = (
            hv[1 - cb, span].astype(F32) + fin[1, hf].astype(F32) + fin[2, hf].astype(F32)
        ).astype(BF)

    for copy in spread(0, h_ref, EARLY) + spread(0, h_ref, LATE):
        copy.wait_send()

    @pl.when(seg == 0)
    def _():
        for copy in spread(1, m_ref, EARLY) + spread(1, m_ref, LATE) + next_door():
            copy.wait_send()

    for rb in (EARLY, LATE):
        for c in (mp, omp):
            for hf in range(NHF):
                for copy in along_y(0, rb, c, hf):
                    copy.wait_send()

                @pl.when(seg == 1)
                def _():
                    for copy in along_y(1, rb, c, hf):
                        copy.wait_send()

        for k in range(1, nc):
            for copy in exchange(rb, k):
                copy.wait_send()

    def drain(t, carry):
        for k in range(1, NY):
            y_copy(t, k).wait_send()
        for i in range(nc):
            @pl.when(zi != i)
            def _():
                give_back(t, i).wait_send()

        return carry

    lax.fori_loop(0, 4, drain, 0)

    def drain_x(z, carry):
        for k in range(1, NX):
            along_x(z, k).wait_send()
        return carry

    lax.fori_loop(0, NZ, drain_x, 0)


def layer(lengths, hidden, memory, w_query, w_key, w_value, w_out, norm_gain, final_gain):
    batch, rows, chunk = hidden.shape
    depth, cols = w_query.shape
    count = NX * NZ * rows
    parts = NH * NY
    nc = NZ // 2
    half = rows // 2
    block = nc * half
    dma = pltpu.SemaphoreType.DMA
    vmem = pl.BlockSpec(memory_space=pltpu.VMEM)
    hbm = pl.BlockSpec(memory_space=pltpu.HBM)
    smem = pl.BlockSpec(memory_space=pltpu.SMEM)
    return pl.pallas_call(
        layer_kernel,
        out_shape=jax.ShapeDtypeStruct((batch, rows, chunk), BF),
        in_specs=[smem] + [hbm] * 6 + [vmem] * 2,
        out_specs=vmem,
        scratch_shapes=[
            pltpu.VMEM((batch, rows, chunk), BF),
            pltpu.VMEM((depth, cols), BF),
            pltpu.VMEM((depth, cols), BF),
            pltpu.VMEM((depth, cols), BF),
            pltpu.VMEM((cols, depth), BF),
            pltpu.VMEM((2, depth), F32),
            pltpu.VMEM((2, 2, parts, rows, chunk), BF),
            pltpu.VMEM((2, rows, cols), F32),
            pltpu.VMEM((2, rows, cols), F32),
            pltpu.VMEM((2, rows, cols), F32),
            pltpu.VMEM((2, 2, rows, LANES), F32),
            pltpu.VMEM((2, nc, half, LANES), BF),
            pltpu.VMEM((2, nc, rows, LANES), BF),
            pltpu.VMEM((NZ, half, LANES), BF),
            pltpu.VMEM((count, LANES), BF),
            pltpu.VMEM((count, LANES), BF),
            pltpu.VMEM((block, count // 2), F32),
            pltpu.VMEM((4, block, LANES), F32),
            pltpu.VMEM((4, block, 2 * LANES), F32),
            pltpu.VMEM((4, nc, half, LANES), BF),
            pltpu.VMEM((4, nc, half, LANES), BF),
            pltpu.VMEM((half, cols), BF),
            pltpu.VMEM((4, NY, NH, half, chunk), BF),
            pltpu.VMEM((4, NH, half, chunk), F32),
            pltpu.VMEM((4, NY, NH, half, chunk), BF),
            pltpu.VMEM((3, 2, half, chunk), BF),
            pltpu.VMEM((3, 2, half, chunk), BF),
            dma((5,)),
            dma((2, 4, 2)),
            dma((2, 4, NY, 2)),
            dma((2, 2, parts, 2)),
            dma((2, 2, nc)),
            dma((NZ,)),
            dma((NX, NZ)),
            dma((NZ, NX)),
            dma((4, nc)),
            dma((4, nc)),
            dma((4, NY)),
            dma((4, NY)),
            dma((3, 2)),
            dma((3, 2)),
        ],
        compiler_params=pltpu.CompilerParams(
            collective_id=1, has_side_effects=True, vmem_limit_bytes=VMEM_LIMIT
        ),
        name="layer",
    )(lengths, hidden, memory, w_query, w_key, w_value, w_out, norm_gain, final_gain)


def body(hidden, memory, w_query, w_key, w_value, w_out, norm_gain, final_gain, lengths):
    out = layer(
        lengths[0], hidden[0], memory[0], w_query[0], w_key[0], w_value[0], w_out[0],
        norm_gain, final_gain.reshape(norm_gain.shape),
    )
    return out[None]


def solution(mesh):
    return jax.shard_map(
        body,
        mesh=mesh,
        in_specs=(
            P("segment", None, "seq", "mp"),
            P("segment", None, "seq", "mp"),
            P("segment", None, "mp"),
            P("segment", None, "mp"),
            P("segment", None, "mp"),
            P("segment", "mp", None),
            P("segment", None),
            P(),
            P("segment", None, None),
        ),
        out_specs=P("segment", None, "seq", "mp"),
        check_vma=False,
    )
```
